512 devices in a mesh: region: 8 (over x, core), owner: 64 (over y, z).
Axes of the slice: x: 4, y: 8, z: 8, core: 2. Of those that a mesh axis runs over, the one named last changes fastest.
Arguments:
- voxels: bfloat16 [8, 64, 1, 256, 1024], P('region', 'owner'), may hold values from -6 to 6
- norm_gain: float32 [1024], replicated, may hold values from 0.5 to 1.5
- qkv_weight: bfloat16 [1024, 3072], P(('region', 'owner')), may hold values from -0.14453125 to 0.14453125
- out_weight: bfloat16 [1024, 1024], P(('region', 'owner')), may hold values from -0.1875 to 0.1875
- neighbours: int32 [8, 64, 1, 8], P('region', 'owner'), may hold values from -1 to 511, as said below
Outputs:
- attended_voxels: bfloat16 [8, 64, 1, 256, 1024], P('region', 'owner')
The draws below stay inside these ranges and needn't reach their ends.
Inputs may be any that keep to these rules, and one draw needn't show every extreme that they name: `neighbours`: each entry is -1 or the number (r * 64 + o) + c of a block c held by the device at region r and owner o, where r and o each differ by at most one from those of the list's own block; a list never names its own block and names no block twice.
All inputs are finite; a program needn't handle non-finite values.
Results may differ from the reference program's by a relative error of at most 0.0057.
Values may be sent and summed in bfloat16 or wider, within the bound.
No kernel may reach another device: no remote copies, remote signals or barrier semaphores. Data moves between devices by JAX's collectives and lax.ppermute only.
A program may use at most 64 MiB of HBM per device.

```python
import jax
import jax.numpy as jnp
from jax import lax

D = 1024
HEADS = 16
HEAD_DIM = 64
S = 256
CAP = 1
NBR = 8
REGIONS = 8
OWNERS = 64


def common_direction(key):
    base = jax.random.normal(jax.random.fold_in(key, 501), (D,), jnp.float32)
    base = jnp.clip(base, -2.2, 2.2)
    base = base - jnp.mean(base)
    return base / jnp.sqrt(jnp.mean(base * base))


def draw_voxels(key, part):
    shape = (REGIONS, OWNERS, CAP, S, D)
    return jax.random.truncated_normal(jax.random.fold_in(key, 504), -6.0, 6.0, shape, jnp.float32).astype(jnp.bfloat16)


def draw_qkv_weight(key, part):
    direction = common_direction(key)
    random_part = jax.random.truncated_normal(jax.random.fold_in(key, 511), -4.0, 4.0, (D, 3 * D), jnp.float32) * D ** (-0.5)
    levels = jax.random.permutation(jax.random.fold_in(key, 512), HEADS).astype(jnp.float32) / (HEADS - 1)
    strength = 7.0 ** levels
    signs = jnp.where(jax.random.bernoulli(jax.random.fold_in(key, 513), 0.5, (HEADS, HEAD_DIM)), 1.0, -1.0)
    pattern = (strength[:, None] * signs).reshape(D) / D
    aligned = direction[:, None] * pattern[None, :]
    blank = jnp.zeros((D, D), jnp.float32)
    return (random_part + jnp.concatenate([aligned, aligned, blank], axis=1)).astype(jnp.bfloat16)


def draw_neighbours(key, part):
    candidate_count = 9 * CAP
    region_ids = jnp.arange(REGIONS, dtype=jnp.int32)[:, None, None, None]
    owner_ids = jnp.arange(OWNERS, dtype=jnp.int32)[None, :, None, None]
    slot_ids = jnp.arange(CAP, dtype=jnp.int32)[None, None, :, None]
    candidate_ids = jnp.arange(candidate_count, dtype=jnp.int32)[None, None, None, :]
    noise = jax.random.randint(jax.random.fold_in(key, 11), (REGIONS, OWNERS, CAP, candidate_count), 0, 1 << 20)
    ranking = noise * 64 + candidate_ids
    ranking = jnp.where(candidate_ids == 4 * CAP + slot_ids, 1 << 30, ranking)
    chosen = jnp.argsort(ranking, axis=-1, stable=True)[..., :NBR].astype(jnp.int32)
    device_pos = chosen // CAP
    other_slot = chosen % CAP
    far_region = region_ids + device_pos // 3 - 1
    far_owner = owner_ids + device_pos % 3 - 1
    inside = (far_region >= 0) & (far_region < REGIONS) & (far_owner >= 0) & (far_owner < OWNERS)
    keeping = jax.random.randint(jax.random.fold_in(key, 12), (REGIONS, OWNERS, CAP, NBR), 0, 10) < 7
    numbers = (far_region * OWNERS + far_owner) * CAP + other_slot
    return jnp.where(inside & keeping, numbers, -1).astype(jnp.int32)


def level_of(rng, extent, cuts, least, high):
    loudness, own = 1.0, jax.random.fold_in(rng, 6)
    for axis_at, blocks in cuts:
        draws = jnp.exp(jax.random.uniform(jax.random.fold_in(own, axis_at), (blocks,), jnp.float32, least / len(cuts), high / len(cuts)))
        loudness = loudness * jnp.repeat(draws, extent[axis_at] // blocks).reshape([-1 if axis == axis_at else 1 for axis in range(len(extent))])
    return loudness


def centred(key, dims, deviation, most, cuts=(), held_as=jnp.bfloat16):
    values = jax.random.normal(key, dims, jnp.float32) * deviation
    if len(cuts) > 0:
        values = level_of(key, dims, cuts, -0.22, 0.18) * values
    return jnp.clip(values, min=-most, max=most).astype(held_as)


def setup_inputs(seed: int = 0) -> dict:
    seeds = jax.random.split(jax.random.key(seed), 6)
    return {
        "voxels": draw_voxels(jax.random.fold_in(seeds[5], 71), 0),
        "norm_gain": jnp.clip(1.0 + 0.1 * jax.random.normal(seeds[1], (D,), jnp.float32), 0.5, 1.5),
        "qkv_weight": draw_qkv_weight(jax.random.fold_in(seeds[5], 71), 0),
        "out_weight": centred(seeds[3], (D, D), D ** -0.5, 0.1875, ((0, 512),)),
        "neighbours": draw_neighbours(jax.random.fold_in(seeds[5], 71), 0),
    }


def layer_norm(inputs, norm_gain):
    widened = inputs.astype(jnp.float32)
    average = lax.optimization_barrier(jnp.mean(widened, axis=-1, keepdims=True))
    spread = lax.optimization_barrier(jnp.mean((widened - average) ** 2, axis=-1, keepdims=True))
    return ((widened - average) * lax.rsqrt(spread + 1e-06) * norm_gain).astype(jnp.bfloat16)

def reference(voxels, norm_gain, qkv_weight, out_weight, neighbours):
    model_width = voxels.shape[-1]
    block_size = voxels.shape[3]
    flat_tokens = voxels.reshape(-1, model_width)
    normed = layer_norm(flat_tokens, norm_gain)
    qkv = jnp.dot(normed, qkv_weight, preferred_element_type=jnp.float32).astype(jnp.bfloat16)
    queries = qkv[:, :model_width].reshape(-1, block_size, HEADS, HEAD_DIM)
    key_table = qkv[:, model_width:2 * model_width].reshape(-1, block_size, HEADS, HEAD_DIM)
    value_table = qkv[:, 2 * model_width:].reshape(-1, block_size, HEADS, HEAD_DIM)
    block_count = queries.shape[0]
    block_ids = jnp.arange(block_count, dtype=jnp.int32)
    key_lists = jnp.concatenate([block_ids[:, None], neighbours.reshape(block_count, NBR).astype(jnp.int32)], axis=1)
    score_scale = HEAD_DIM ** (-0.5)

    def attend(operands):
        query_block, key_list = operands
        present = key_list >= 0
        clamped = jnp.where(present, key_list, 0).astype(jnp.int32)
        key_rows = key_table[clamped].reshape(-1, HEADS, HEAD_DIM).astype(jnp.float32)
        value_rows = value_table[clamped].reshape(-1, HEADS, HEAD_DIM).astype(jnp.float32)
        scores = jnp.einsum('shd,khd->hsk', query_block.astype(jnp.float32), key_rows) * score_scale
        key_mask = jnp.repeat(present, block_size)
        scores = jnp.where(key_mask[None, None, :], scores, -1e+30)
        attn_probs = jax.nn.softmax(scores, axis=-1).astype(jnp.bfloat16)
        attended = jnp.einsum('hsk,khd->shd', attn_probs.astype(jnp.float32), value_rows)
        return attended.reshape(block_size, model_width).astype(jnp.bfloat16)
    mixed = lax.map(attend, (queries, key_lists))
    projected = jnp.dot(mixed.reshape(-1, model_width), out_weight, preferred_element_type=jnp.float32)
    result = flat_tokens.astype(jnp.float32) + projected
    return result.astype(jnp.bfloat16).reshape(voxels.shape)
```

```python
import functools

import jax
import jax.numpy as jnp
from jax import lax
from jax.experimental import pallas as pl
from jax.experimental.pallas import tpu as pltpu
from jax.sharding import Mesh, PartitionSpec as P


HEAD_DIM = 64
LOG2E = 1.4426950408889634
LINE = ("x", "c")
PLANE = ("y", "z")
BF16 = jnp.bfloat16
F32 = jnp.float32


def norm_kernel(tokens_ref, gain_ref, out_ref):
    widened = tokens_ref[...].astype(F32)
    average = jnp.mean(widened, axis=-1, keepdims=True)
    centred = widened - average
    spread = jnp.mean(centred * centred, axis=-1, keepdims=True)
    out_ref[...] = (centred * lax.rsqrt(spread + 1e-06) * gain_ref[...]).astype(BF16)


def layer_norm(tokens, norm_gain):
    return pl.pallas_call(
        norm_kernel,
        grid=(2,),
        in_specs=[
            pl.BlockSpec((128, 1024), lambda i: (i, 0)),
            pl.BlockSpec((1, 1024), lambda i: (0, 0)),
        ],
        out_specs=pl.BlockSpec((128, 1024), lambda i: (i, 0)),
        out_shape=jax.ShapeDtypeStruct((256, 1024), BF16),
        name="layer_norm",
    )(tokens, norm_gain.reshape(1, 1024))


def shift(value, axis, step):
    n = lax.axis_size(axis)
    return lax.ppermute(value, axis, [(i, (i + step) % n) for i in range(n)])


def from_everyone(value, axes):
    n = lax.axis_size(axes)
    return lax.all_to_all(jnp.broadcast_to(value[None], (n, *value.shape)), axes, 0, 0, tiled=True)


def region_of(slot, x, c):
    parity, place = (slot // 4, slot % 4)
    step = jnp.where(place == 0, 0, jnp.where(place == 1, 3, place - 1))
    return 2 * ((x + step) % 4) + (c + parity) % 2


def slot_of(region, x, c):
    step = (region // 2 - x + 4) % 4
    place = jnp.where(step == 0, 0, jnp.where(step == 3, 1, step + 1))
    return 4 * ((region % 2 + c) % 2) + place


def qkv_kernel(mine_ref, other_ref, weight_ref, kv_ref, query_ref, value_weight):
    slot = pl.program_id(0)

    @pl.when(slot == 0)
    def _():
        value_weight[...] = weight_ref[:, 256:384].T

    def project(tokens):
        both = jnp.dot(tokens, weight_ref[:, :256], preferred_element_type=F32).astype(BF16)
        kv_ref[0, 0:256, :] = both[:, :128]
        query_ref[0] = both[:, 128:]
        values = lax.dot_general(
            value_weight[...], tokens, (((1,), (1,)), ((), ())), preferred_element_type=F32
        ).astype(BF16)
        kv_ref[0, 256:384, :] = values[:, :128]
        kv_ref[0, 384:512, :] = values[:, 128:]

    @pl.when(slot < 4)
    def _():
        project(mine_ref[...])

    @pl.when(slot >= 4)
    def _():
        project(other_ref[...])


def project_qkv(mine, other, weight):
    return pl.pallas_call(
        qkv_kernel,
        grid=(8,),
        in_specs=[
            pl.BlockSpec((256, 1024), lambda s: (jnp.minimum(s, 3), 0)),
            pl.BlockSpec((256, 1024), lambda s: (jnp.maximum(s - 4, 0), 0)),
            pl.BlockSpec((1024, 384), lambda s: (0, 0)),
        ],
        out_specs=[
            pl.BlockSpec((1, 512, 128), lambda s: (s, 0, 0)),
            pl.BlockSpec((1, 256, 128), lambda s: (s, 0, 0)),
        ],
        out_shape=[
            jax.ShapeDtypeStruct((8, 512, 128), BF16),
            jax.ShapeDtypeStruct((8, 256, 128), BF16),
        ],
        scratch_shapes=[pltpu.VMEM((128, 1024), BF16)],
        name="project_qkv",
    )(mine, other, weight)


FACTOR = HEAD_DIM ** (-0.5) * LOG2E


def near_places(table, refs):
    x, c = (table[72], table[73])
    region = region_of(pl.program_id(0), x, c)
    places = []
    for side, ref in refs:
        for step in range(3):
            near = jnp.clip(region + step - 1, 0, 7)
            flag = table[region * 9 + step * 3 + side]
            places.append((ref, slot_of(near, x, c), jnp.where(flag > 0, 0.0, 1e30).astype(F32)))
    return places


def score_places(places, query, cols, score_ref):
    tops = []
    for entry, (ref, slot, penalty) in enumerate(places):
        scores = lax.dot_general(
            ref[slot, 0:256, cols], query, (((1,), (1,)), ((), ())), preferred_element_type=F32
        )
        score_ref[entry] = scores
        tops.append(jnp.max(scores, axis=0, keepdims=True) - penalty)
    return functools.reduce(jnp.maximum, tops) * FACTOR


def mix_places(places, head, top, score_ref):
    ones = jnp.ones((16, 256), BF16)
    totals = []
    for entry, (ref, slot, penalty) in enumerate(places):
        weights = jnp.exp2(score_ref[entry] * FACTOR - (top + penalty)).astype(BF16)
        first = ref[slot, 256 + head * 64 : 320 + head * 64, :]
        second = ref[slot, 384 + head * 64 : 448 + head * 64, :]
        values = jnp.concatenate([jnp.concatenate([first, second], axis=1), ones], axis=0)
        totals.append(jnp.dot(values, weights, preferred_element_type=F32))
    return functools.reduce(jnp.add, totals)


def attend_own_kernel(table, query_ref, own_ref, total_ref, top_ref, score_ref):
    places = near_places(table, [(1, own_ref)])
    for head in range(2):
        cols = slice(head * 64, head * 64 + 64)
        top = score_places(places, query_ref[0, :, cols], cols, score_ref.at[head])
        total_ref[0, head] = mix_places(places, head, top, score_ref.at[head])
        top_ref[0, head] = jnp.broadcast_to(top, (8, 256))


def attend_own(table, queries, own):
    return pl.pallas_call(
        attend_own_kernel,
        grid_spec=pltpu.PrefetchScalarGridSpec(
            num_scalar_prefetch=1,
            grid=(8,),
            in_specs=[
                pl.BlockSpec((1, 256, 128), lambda s, t: (s, 0, 0)),
                pl.BlockSpec(memory_space=pltpu.VMEM),
            ],
            out_specs=[
                pl.BlockSpec((1, 2, 80, 256), lambda s, t: (s, 0, 0, 0)),
                pl.BlockSpec((1, 2, 8, 256), lambda s, t: (s, 0, 0, 0)),
            ],
            scratch_shapes=[pltpu.VMEM((2, 3, 256, 256), F32)],
        ),
        out_shape=[
            jax.ShapeDtypeStruct((8, 2, 80, 256), F32),
            jax.ShapeDtypeStruct((8, 2, 8, 256), F32),
        ],
        name="attend_own",
    )(table, queries, own)


def attend_kernel(
    table, query_ref, low_ref, high_ref, own_total_ref, own_top_ref, out_ref, score_ref
):
    places = near_places(table, [(0, low_ref), (2, high_ref)])
    for head in range(2):
        cols = slice(head * 64, head * 64 + 64)
        own_top = own_top_ref[0, head, 0:1]
        top = score_places(places, query_ref[0, :, cols], cols, score_ref.at[head])
        top = jnp.maximum(top, own_top)
        total = own_total_ref[0, head] * jnp.exp2(own_top - top)
        total += mix_places(places, head, top, score_ref.at[head])
        out_ref[0, cols, :] = (total[:64] / total[64:65]).astype(BF16)


def attend(table, queries, low, high, own_total, own_top):
    whole = pl.BlockSpec(memory_space=pltpu.VMEM)
    return pl.pallas_call(
        attend_kernel,
        grid_spec=pltpu.PrefetchScalarGridSpec(
            num_scalar_prefetch=1,
            grid=(8,),
            in_specs=[
                pl.BlockSpec((1, 256, 128), lambda s, t: (s, 0, 0)),
                whole,
                whole,
                pl.BlockSpec((1, 2, 80, 256), lambda s, t: (s, 0, 0, 0)),
                pl.BlockSpec((1, 2, 8, 256), lambda s, t: (s, 0, 0, 0)),
            ],
            out_specs=pl.BlockSpec(
                (1, 128, 256), lambda s, t: (region_of(s, t[72], t[73]), 0, 0)
            ),
            scratch_shapes=[pltpu.VMEM((2, 6, 256, 256), F32)],
        ),
        out_shape=jax.ShapeDtypeStruct((8, 128, 256), BF16),
        name="attend",
    )(table, queries, low, high, own_total, own_top)


def output_kernel(table, mixed_ref, mine_ref, other_ref, voxels_ref, out_ref):
    x, c = (table[72], table[73])
    total = voxels_ref[...].astype(F32)
    for slot in range(8):
        rows = (mine_ref, other_ref)[slot // 4][slot % 4 * 128 : slot % 4 * 128 + 128, :]
        heads = mixed_ref[region_of(slot, x, c)]
        total += lax.dot_general(
            heads, rows, (((0,), (0,)), ((), ())), preferred_element_type=F32
        )
    out_ref[...] = total.astype(BF16)


def project_out(table, mixed, mine, other, voxels):
    return pl.pallas_call(
        output_kernel,
        grid_spec=pltpu.PrefetchScalarGridSpec(
            num_scalar_prefetch=1,
            grid=(2,),
            in_specs=[
                pl.BlockSpec((8, 128, 256), lambda n, t: (0, 0, 0)),
                pl.BlockSpec((512, 512), lambda n, t: (0, n)),
                pl.BlockSpec((512, 512), lambda n, t: (0, n)),
                pl.BlockSpec((256, 512), lambda n, t: (0, n)),
            ],
            out_specs=pl.BlockSpec((256, 512), lambda n, t: (0, n)),
        ),
        out_shape=jax.ShapeDtypeStruct((256, 1024), BF16),
        name="project_out",
    )(table, mixed, mine, other, voxels)


def gathered_line(value):
    pieces = [value]
    for step in (1, -1, 2):
        pieces.append(shift(value, "x", step))
    mine = jnp.concatenate(pieces, axis=0)
    return (mine, shift(mine, "c", 1))


def layer(voxels, norm_gain, qkv_weight, out_weight, neighbours):
    x, c, y, z = (lax.axis_index(a) for a in ("x", "c", "y", "z"))
    region, owner = (2 * x + c, 8 * y + z)
    tokens = voxels.reshape(256, 1024)
    ids = neighbours.reshape(1, 8)
    entry = jnp.arange(128, dtype=jnp.int32)[:, None]
    near_region = region + entry // 3 - 1
    near_owner = owner + entry % 3 - 1
    inside = (
        (entry < 9) & (near_region >= 0) & (near_region < 8) & (near_owner >= 0) & (near_owner < 64)
    )
    listed = jnp.any((ids == near_region * 64 + near_owner) & inside, axis=1) | (entry[:, 0] == 4)

    normed = layer_norm(tokens, norm_gain)
    mine, other = gathered_line(normed)

    parts = qkv_weight.reshape(2, 3, 8, 128)
    parts = jnp.stack([parts[:, 1], parts[:, 0], parts[:, 2]], axis=2)
    parts = parts.transpose(1, 0, 2, 3).reshape(8, 2, 384)
    flags = jnp.broadcast_to(listed.astype(BF16)[None, None], (8, 2, 128))
    parts = jnp.concatenate([parts, flags], axis=2)
    swapped = lax.all_to_all(parts, LINE, 0, 0, tiled=True)
    table = jnp.concatenate([
        swapped[:, 0, 384:393].astype(jnp.int32).reshape(72),
        jnp.stack([x, c]).astype(jnp.int32),
    ])
    weight = from_everyone(swapped[:, :, :384].reshape(16, 384), PLANE)
    weight = weight.reshape(64, 8, 2, 384).transpose(1, 0, 2, 3).reshape(1024, 384)

    own, queries = project_qkv(mine, other, weight)
    line = [(i, i + 1) for i in range(63)]
    low = lax.ppermute(own, PLANE, line)
    high = lax.ppermute(own, PLANE, [(j, i) for i, j in line])
    own_total, own_top = attend_own(table, queries, own)

    out_rows, _ = lax.optimization_barrier((out_weight, queries))
    out_rows = from_everyone(out_rows, "z").reshape(16, 1024)
    out_rows = from_everyone(out_rows, "y").reshape(128, 1024)
    out_mine, out_other = gathered_line(out_rows)

    mixed = attend(table, queries, low, high, own_total, own_top)
    mixed = lax.all_to_all(mixed, LINE, 0, 0, tiled=True)
    result = project_out(table, mixed, out_mine, out_other, tokens)
    return result.reshape(voxels.shape)


def solution(mesh):
    fine = Mesh(mesh.devices.reshape(4, 2, 8, 8), ("x", "c", "y", "z"))
    return jax.shard_map(
        layer,
        mesh=fine,
        in_specs=(
            P(LINE, PLANE, None, None, None),
            P(),
            P((*LINE, *PLANE), None),
            P((*LINE, *PLANE), None),
            P(LINE, PLANE, None, None),
        ),
        out_specs=P(LINE, PLANE, None, None, None),
        check_vma=False,
    )
```

```python
import functools

import jax
import jax.numpy as jnp
from jax import lax
from jax.experimental import pallas as pl
from jax.experimental.pallas import tpu as pltpu
from jax.sharding import Mesh, PartitionSpec as P


HEAD_DIM = 64
FACTOR = HEAD_DIM ** (-0.5) * 1.4426950408889634
LINE = ("x", "c")
PLANE = ("y", "z")
BF16 = jnp.bfloat16
F32 = jnp.float32


def norm_kernel(tokens_ref, gain_ref, out_ref):
    widened = tokens_ref[...].astype(F32)
    average = jnp.mean(widened, axis=-1, keepdims=True)
    centred = widened - average
    spread = jnp.mean(centred * centred, axis=-1, keepdims=True)
    out_ref[...] = (centred * lax.rsqrt(spread + 1e-06) * gain_ref[...]).astype(BF16)


def layer_norm(tokens, norm_gain):
    return pl.pallas_call(
        norm_kernel,
        grid=(2,),
        in_specs=[
            pl.BlockSpec((128, 1024), lambda i: (i, 0)),
            pl.BlockSpec((1, 1024), lambda i: (0, 0)),
        ],
        out_specs=pl.BlockSpec((128, 1024), lambda i: (i, 0)),
        out_shape=jax.ShapeDtypeStruct((256, 1024), BF16),
        name="layer_norm",
    )(tokens, norm_gain.reshape(1, 1024))


def shift(value, axis, step):
    n = lax.axis_size(axis)
    return lax.ppermute(value, axis, [(i, (i + step) % n) for i in range(n)])


def from_everyone(value, axes):
    n = lax.axis_size(axes)
    return lax.all_to_all(jnp.broadcast_to(value[None], (n, *value.shape)), axes, 0, 0, tiled=True)


def region_of(slot, x, c):
    parity, place = (slot // 4, slot % 4)
    step = jnp.where(place == 0, 0, jnp.where(place == 1, 3, place - 1))
    return 2 * ((x + step) % 4) + (c + parity) % 2


def slot_of(region, x, c):
    step = (region // 2 - x + 4) % 4
    place = jnp.where(step == 0, 0, jnp.where(step == 3, 1, step + 1))
    return 4 * ((region % 2 + c) % 2) + place


def qkv_kernel(mine_ref, other_ref, weight_ref, kv_ref, query_ref):
    def project(tokens_ref):
        projected = jnp.dot(tokens_ref[...], weight_ref[...], preferred_element_type=F32)
        for block in range(4):
            rows = slice(block * 256, block * 256 + 256)
            kv_ref[block, 0:256, :] = projected[rows, :128].astype(BF16)
            values = projected[rows, 128:256].astype(BF16).T
            kv_ref[block, 256:384, :] = values[:, :128]
            kv_ref[block, 384:512, :] = values[:, 128:]
            query_ref[block] = (projected[rows, 256:] * FACTOR).astype(BF16)

    @pl.when(pl.program_id(0) == 0)
    def _():
        project(mine_ref)

    @pl.when(pl.program_id(0) == 1)
    def _():
        project(other_ref)


def project_qkv(mine, other, weight):
    return pl.pallas_call(
        qkv_kernel,
        grid=(2,),
        in_specs=[
            pl.BlockSpec((1024, 1024), lambda s: (0, 0)),
            pl.BlockSpec((1024, 1024), lambda s: (0, 0)),
            pl.BlockSpec((1024, 384), lambda s: (0, 0)),
        ],
        out_specs=[
            pl.BlockSpec((4, 512, 128), lambda s: (s, 0, 0)),
            pl.BlockSpec((4, 256, 128), lambda s: (s, 0, 0)),
        ],
        out_shape=[
            jax.ShapeDtypeStruct((8, 512, 128), BF16),
            jax.ShapeDtypeStruct((8, 256, 128), BF16),
        ],
        name="project_qkv",
    )(mine, other, weight)


def near_places(table, slot, refs):
    x, c = (table[72], table[73])
    region = region_of(slot, x, c)
    places = []
    for side, ref in refs:
        for step in range(3):
            near = jnp.clip(region + step - 1, 0, 7)
            flag = table[region * 9 + step * 3 + side]
            places.append((ref, slot_of(near, x, c), jnp.where(flag > 0, 0.0, 1e30).astype(F32)))
    return places


def run_units(table, query_ref, refs, score_ref, weight_ref, known_top, finish):
    lanes = lax.broadcasted_iota(jnp.int32, (256, 128), 1)
    units = []
    for place in range(2):
        places = near_places(table, pl.program_id(0) * 2 + place, refs)
        for head in range(2):
            inside = (lanes >= head * 64) & (lanes < head * 64 + 64)
            query = jnp.where(inside, query_ref[place], jnp.zeros((), BF16))
            units.append((place, head, places, query))
    count = len(units[0][2])
    ones = jnp.ones((16, count * 256), BF16)
    tops = []
    for turn in range(5):
        column_tops = []
        for entry in range(count):
            rows = slice(entry * 256, entry * 256 + 256)
            if turn < 4:
                _, _, places, query = units[turn]
                ref, slot, penalty = places[entry]
                scores = lax.dot_general(
                    ref[slot, 0:256, :], query, (((1,), (1,)), ((), ())),
                    preferred_element_type=F32,
                )
                score_ref[turn % 2, rows] = scores
                column_tops.append(jnp.max(scores, axis=0, keepdims=True) - penalty)
            if turn > 0:
                penalty = units[turn - 1][2][entry][2]
                weight_ref[(turn - 1) % 2, rows] = jnp.exp2(
                    score_ref[(turn - 1) % 2, rows] - (tops[-1] + penalty)
                ).astype(BF16)
        if turn > 0:
            place, head, places, _ = units[turn - 1]
            halves = []
            for ref, slot, _ in places:
                halves.append(ref[slot, 256 + head * 64 : 320 + head * 64, :])
                halves.append(ref[slot, 384 + head * 64 : 448 + head * 64, :])
            values = jnp.concatenate([jnp.concatenate(halves, axis=1), ones], axis=0)
            total = jnp.dot(values, weight_ref[(turn - 1) % 2], preferred_element_type=F32)
            finish(place, head, tops[-1], total)
        if turn < 4:
            top = functools.reduce(jnp.maximum, column_tops)
            if known_top is not None:
                top = jnp.maximum(top, known_top(*units[turn][:2]))
            tops.append(top)


def attend_own_kernel(
    table, query_ref, own_ref, total_ref, top_ref, score_ref, weight_ref
):
    def finish(place, head, top, total):
        total_ref[place, head] = total
        top_ref[place, head] = jnp.broadcast_to(top, (8, 256))

    run_units(table, query_ref, [(1, own_ref)], score_ref, weight_ref, None, finish)


WHOLE = pl.BlockSpec((8, 512, 128), lambda s, t: (0, 0, 0), pipeline_mode=pl.Buffered(1))


def attend_own(table, queries, own):
    return pl.pallas_call(
        attend_own_kernel,
        grid_spec=pltpu.PrefetchScalarGridSpec(
            num_scalar_prefetch=1,
            grid=(4,),
            in_specs=[pl.BlockSpec((2, 256, 128), lambda s, t: (s, 0, 0)), WHOLE],
            out_specs=[
                pl.BlockSpec((2, 2, 80, 256), lambda s, t: (s, 0, 0, 0)),
                pl.BlockSpec((2, 2, 8, 256), lambda s, t: (s, 0, 0, 0)),
            ],
            scratch_shapes=[pltpu.VMEM((2, 768, 256), F32), pltpu.VMEM((2, 768, 256), BF16)],
        ),
        out_shape=[
            jax.ShapeDtypeStruct((8, 2, 80, 256), F32),
            jax.ShapeDtypeStruct((8, 2, 8, 256), F32),
        ],
        name="attend_own",
    )(table, queries, own)


def attend_kernel(
    table, query_ref, low_ref, high_ref, own_total_ref, own_top_ref, out_ref, score_ref, weight_ref
):
    def known_top(place, head):
        return own_top_ref[place, head, 0:1]

    def finish(place, head, top, total):
        total += own_total_ref[place, head] * jnp.exp2(known_top(place, head) - top)
        region = region_of(pl.program_id(0) * 2 + place, table[72], table[73])
        out_ref[region, head * 64 : head * 64 + 64, :] = (total[:64] / total[64:65]).astype(BF16)

    run_units(table, query_ref, [(0, low_ref), (2, high_ref)], score_ref, weight_ref, known_top, finish)


def attend(table, queries, low, high, own_total, own_top):
    return pl.pallas_call(
        attend_kernel,
        grid_spec=pltpu.PrefetchScalarGridSpec(
            num_scalar_prefetch=1,
            grid=(4,),
            in_specs=[
                pl.BlockSpec((2, 256, 128), lambda s, t: (s, 0, 0)),
                WHOLE,
                WHOLE,
                pl.BlockSpec((2, 2, 80, 256), lambda s, t: (s, 0, 0, 0)),
                pl.BlockSpec((2, 2, 8, 256), lambda s, t: (s, 0, 0, 0)),
            ],
            out_specs=pl.BlockSpec((8, 128, 256), lambda s, t: (0, 0, 0)),
            scratch_shapes=[pltpu.VMEM((2, 1536, 256), F32), pltpu.VMEM((2, 1536, 256), BF16)],
        ),
        out_shape=jax.ShapeDtypeStruct((8, 128, 256), BF16),
        name="attend",
    )(table, queries, low, high, own_total, own_top)


def output_kernel(table, mixed_ref, mine_ref, other_ref, voxels_ref, out_ref):
    mixed = mixed_ref[...].T
    for pair in range(4):
        ref = (mine_ref, other_ref)[pair // 2]
        slots = (2 * pair, 2 * pair + 1)
        weight = jnp.concatenate([ref[slot % 4] for slot in slots], axis=1)
        projected = jnp.dot(mixed, weight, preferred_element_type=F32)
        for place, slot in enumerate(slots):
            start = pl.multiple_of(region_of(slot, table[72], table[73]) * 128, 128)
            cols = pl.ds(start, 128)
            part = projected[:, place * 128 : place * 128 + 128]
            out_ref[:, cols] = (voxels_ref[:, cols].astype(F32) + part).astype(BF16)


def project_out(table, mixed, mine, other, voxels):
    return pl.pallas_call(
        output_kernel,
        grid_spec=pltpu.PrefetchScalarGridSpec(
            num_scalar_prefetch=1,
            grid=(1,),
            in_specs=[
                pl.BlockSpec((1024, 256), lambda n, t: (0, 0)),
                pl.BlockSpec((4, 1024, 128), lambda n, t: (0, 0, 0)),
                pl.BlockSpec((4, 1024, 128), lambda n, t: (0, 0, 0)),
                pl.BlockSpec((256, 1024), lambda n, t: (0, 0)),
            ],
            out_specs=pl.BlockSpec((256, 1024), lambda n, t: (0, 0)),
        ),
        out_shape=jax.ShapeDtypeStruct((256, 1024), BF16),
        name="project_out",
    )(table, mixed, mine, other, voxels)


def gathered_line(value):
    pieces = [value]
    for step in (1, -1, 2):
        pieces.append(shift(value, "x", step))
    mine = jnp.concatenate(pieces, axis=0)
    return (mine, shift(mine, "c", 1))


def layer(voxels, norm_gain, qkv_weight, out_weight, neighbours):
    x, c, y, z = (lax.axis_index(a) for a in ("x", "c", "y", "z"))
    region, owner = (2 * x + c, 8 * y + z)
    tokens = voxels.reshape(256, 1024)
    ids = neighbours.reshape(1, 8)
    entry = jnp.arange(128, dtype=jnp.int32)[:, None]
    near_region = region + entry // 3 - 1
    near_owner = owner + entry % 3 - 1
    inside = (
        (entry < 9) & (near_region >= 0) & (near_region < 8) & (near_owner >= 0) & (near_owner < 64)
    )
    listed = jnp.any((ids == near_region * 64 + near_owner) & inside, axis=1) | (entry[:, 0] == 4)

    normed = layer_norm(tokens, norm_gain)
    mine, other = gathered_line(normed)

    parts = qkv_weight.reshape(2, 3, 8, 128)
    flags = jnp.broadcast_to(listed.astype(BF16)[None, None], (2, 8, 128))
    parts = [parts[:, 1], parts[:, 2], parts[:, 0], out_weight.reshape(2, 8, 128), flags]
    parts = jnp.stack(parts, axis=2).transpose(1, 0, 2, 3).reshape(8, 2, 640)
    swapped = lax.all_to_all(parts, LINE, 0, 0, tiled=True)
    table = jnp.concatenate([
        swapped[:, 0, 512:521].astype(jnp.int32).reshape(72),
        jnp.stack([x, c]).astype(jnp.int32),
    ])

    def in_row_order(weight):
        width = weight.shape[-1]
        return weight.reshape(64, 8, 2, width).transpose(1, 0, 2, 3).reshape(1024, width)

    weight = from_everyone(swapped[:, :, :384].reshape(16, 384), PLANE)
    own, queries = project_qkv(mine, other, in_row_order(weight))
    line = [(i, i + 1) for i in range(63)]
    low = lax.ppermute(own, PLANE, line)
    high = lax.ppermute(own, PLANE, [(j, i) for i, j in line])

    out_part, _ = lax.optimization_barrier((swapped[:, :, 384:512], queries))
    out_part = from_everyone(out_part.reshape(16, 128), PLANE)
    own_total, own_top = attend_own(table, queries, own)
    out_part = in_row_order(out_part)
    out_mine, out_other = gathered_line(out_part)
    mixed = attend(table, queries, low, high, own_total, own_top)
    mixed = lax.all_to_all(mixed, LINE, 0, 0, tiled=True).reshape(1024, 256)
    out_mine, out_other = (part.reshape(4, 1024, 128) for part in (out_mine, out_other))
    result = project_out(table, mixed, out_mine, out_other, tokens)
    return result.reshape(voxels.shape)


def solution(mesh):
    fine = Mesh(mesh.devices.reshape(4, 2, 8, 8), ("x", "c", "y", "z"))
    return jax.shard_map(
        layer,
        mesh=fine,
        in_specs=(
            P(LINE, PLANE, None, None, None),
            P(),
            P((*LINE, *PLANE), None),
            P((*LINE, *PLANE), None),
            P(LINE, PLANE, None, None),
        ),
        out_specs=P(LINE, PLANE, None, None, None),
        check_vma=False,
    )
```

```python
import functools

import jax
import jax.numpy as jnp
from jax import lax
from jax.experimental import pallas as pl
from jax.experimental.pallas import tpu as pltpu
from jax.sharding import Mesh, PartitionSpec as P


HEAD_DIM = 64
FACTOR = HEAD_DIM ** (-0.5) * 1.4426950408889634
LINE = ("x", "c")
PLANE = ("y", "z")
BF16 = jnp.bfloat16
F32 = jnp.float32


def norm_kernel(tokens_ref, gain_ref, out_ref):
    widened = tokens_ref[...].astype(F32)
    average = jnp.mean(widened, axis=-1, keepdims=True)
    centred = widened - average
    spread = jnp.mean(centred * centred, axis=-1, keepdims=True)
    out_ref[...] = (centred * lax.rsqrt(spread + 1e-06) * gain_ref[...]).astype(BF16)


def layer_norm(tokens, norm_gain):
    return pl.pallas_call(
        norm_kernel,
        grid=(2,),
        in_specs=[
            pl.BlockSpec((128, 1024), lambda i: (i, 0)),
            pl.BlockSpec((1, 1024), lambda i: (0, 0)),
        ],
        out_specs=pl.BlockSpec((128, 1024), lambda i: (i, 0)),
        out_shape=jax.ShapeDtypeStruct((256, 1024), BF16),
        name="layer_norm",
    )(tokens, norm_gain.reshape(1, 1024))


def shift(value, axis, step):
    n = lax.axis_size(axis)
    return lax.ppermute(value, axis, [(i, (i + step) % n) for i in range(n)])


def from_everyone(value, axes):
    n = lax.axis_size(axes)
    return lax.all_to_all(jnp.broadcast_to(value[None], (n, *value.shape)), axes, 0, 0, tiled=True)


def region_of(slot, x, c):
    parity, place = (slot // 4, slot % 4)
    step = jnp.where(place == 0, 0, jnp.where(place == 1, 3, place - 1))
    return 2 * ((x + step) % 4) + (c + parity) % 2


def slot_of(region, x, c):
    step = (region // 2 - x + 4) % 4
    place = jnp.where(step == 0, 0, jnp.where(step == 3, 1, step + 1))
    return 4 * ((region % 2 + c) % 2) + place


WHOLE = pl.BlockSpec(memory_space=pltpu.VMEM)


def on_chip(value):
    return pltpu.with_memory_space_constraint(value, pltpu.VMEM)


def qkv_kernel(mine_ref, other_ref, gathered_ref, kv_ref, query_ref, weight_ref):
    def project(tokens_ref):
        projected = jnp.dot(tokens_ref[...], weight_ref[...], preferred_element_type=F32)
        for block in range(4):
            rows = slice(block * 256, block * 256 + 256)
            kv_ref[block, 0:256, :] = projected[rows, :128].astype(BF16)
            values = projected[rows, 128:256].astype(BF16).T
            kv_ref[block, 256:384, :] = values[:, :128]
            kv_ref[block, 384:512, :] = values[:, 128:]
            query_ref[block] = (projected[rows, 256:] * FACTOR).astype(BF16)

    @pl.when(pl.program_id(0) == 0)
    def _():
        for region in range(8):
            for y in range(8):
                row = region * 128 + y * 16
                weight_ref[row : row + 16] = gathered_ref[y, region * 16 : region * 16 + 16]
        project(mine_ref)

    @pl.when(pl.program_id(0) == 1)
    def _():
        project(other_ref)


def project_qkv(mine, other, weight):
    return pl.pallas_call(
        qkv_kernel,
        grid=(2,),
        in_specs=[
            pl.BlockSpec(memory_space=pltpu.VMEM),
            pl.BlockSpec((1024, 1024), lambda s: (0, 0)),
            pl.BlockSpec(memory_space=pltpu.VMEM),
        ],
        out_specs=[
            pl.BlockSpec((4, 512, 128), lambda s: (s, 0, 0)),
            pl.BlockSpec((4, 256, 128), lambda s: (s, 0, 0)),
        ],
        out_shape=[
            jax.ShapeDtypeStruct((8, 512, 128), BF16),
            jax.ShapeDtypeStruct((8, 256, 128), BF16),
        ],
        scratch_shapes=[pltpu.VMEM((1024, 384), BF16)],
        name="project_qkv",
    )(on_chip(mine), other, on_chip(weight))


def near_places(table, slot, refs):
    x, c = (table[72], table[73])
    region = region_of(slot, x, c)
    places = []
    for side, ref in refs:
        for step in range(3):
            near = jnp.clip(region + step - 1, 0, 7)
            flag = table[region * 9 + step * 3 + side]
            places.append((ref, slot_of(near, x, c), jnp.where(flag > 0, 0.0, 1e30).astype(F32)))
    return places


def run_units(table, query_ref, refs, score_ref, weight_ref, known_top, finish):
    lanes = lax.broadcasted_iota(jnp.int32, (256, 128), 1)
    units = []
    for place in range(2):
        places = near_places(table, pl.program_id(0) * 2 + place, refs)
        for head in range(2):
            inside = (lanes >= head * 64) & (lanes < head * 64 + 64)
            query = jnp.where(inside, query_ref[place], jnp.zeros((), BF16))
            units.append((place, head, places, query))
    count = len(units[0][2])
    ones = jnp.ones((16, count * 256), BF16)
    tops = []
    for turn in range(5):
        column_tops = []
        for entry in range(count):
            rows = slice(entry * 256, entry * 256 + 256)
            if turn < 4:
                _, _, places, query = units[turn]
                ref, slot, penalty = places[entry]
                scores = lax.dot_general(
                    ref[slot, 0:256, :], query, (((1,), (1,)), ((), ())),
                    preferred_element_type=F32,
                )
                score_ref[turn % 2, rows] = scores
                column_tops.append(jnp.max(scores, axis=0, keepdims=True) - penalty)
            if turn > 0:
                penalty = units[turn - 1][2][entry][2]
                weight_ref[(turn - 1) % 2, rows] = jnp.exp2(
                    score_ref[(turn - 1) % 2, rows] - (tops[-1] + penalty)
                ).astype(BF16)
        if turn > 0:
            place, head, places, _ = units[turn - 1]
            halves = []
            for ref, slot, _ in places:
                halves.append(ref[slot, 256 + head * 64 : 320 + head * 64, :])
                halves.append(ref[slot, 384 + head * 64 : 448 + head * 64, :])
            values = jnp.concatenate([jnp.concatenate(halves, axis=1), ones], axis=0)
            total = jnp.dot(values, weight_ref[(turn - 1) % 2], preferred_element_type=F32)
            finish(place, head, tops[-1], total)
        if turn < 4:
            top = functools.reduce(jnp.maximum, column_tops)
            if known_top is not None:
                top = jnp.maximum(top, known_top(*units[turn][:2]))
            tops.append(top)


def attend_own_kernel(
    table, query_ref, own_ref, total_ref, top_ref, score_ref, weight_ref
):
    def finish(place, head, top, total):
        total_ref[place, head] = total
        top_ref[place, head] = jnp.broadcast_to(top, (8, 256))

    run_units(table, query_ref, [(1, own_ref)], score_ref, weight_ref, None, finish)


def attend_own(table, queries, own):
    return pl.pallas_call(
        attend_own_kernel,
        grid_spec=pltpu.PrefetchScalarGridSpec(
            num_scalar_prefetch=1,
            grid=(4,),
            in_specs=[pl.BlockSpec((2, 256, 128), lambda s, t: (s, 0, 0)), WHOLE],
            out_specs=[
                pl.BlockSpec((2, 2, 80, 256), lambda s, t: (s, 0, 0, 0)),
                pl.BlockSpec((2, 2, 8, 256), lambda s, t: (s, 0, 0, 0)),
            ],
            scratch_shapes=[pltpu.VMEM((2, 768, 256), F32), pltpu.VMEM((2, 768, 256), BF16)],
        ),
        out_shape=[
            jax.ShapeDtypeStruct((8, 2, 80, 256), F32),
            jax.ShapeDtypeStruct((8, 2, 8, 256), F32),
        ],
        name="attend_own",
    )(table, queries, own)


def attend_kernel(
    table, query_ref, low_ref, high_ref, own_total_ref, own_top_ref, out_ref, score_ref, weight_ref
):
    def known_top(place, head):
        return own_top_ref[place, head, 0:1]

    def finish(place, head, top, total):
        total += own_total_ref[place, head] * jnp.exp2(known_top(place, head) - top)
        region = region_of(pl.program_id(0) * 2 + place, table[72], table[73])
        out_ref[region, head * 64 : head * 64 + 64, :] = (total[:64] / total[64:65]).astype(BF16)

    run_units(table, query_ref, [(0, low_ref), (2, high_ref)], score_ref, weight_ref, known_top, finish)


def attend(table, queries, low, high, own_total, own_top):
    return pl.pallas_call(
        attend_kernel,
        grid_spec=pltpu.PrefetchScalarGridSpec(
            num_scalar_prefetch=1,
            grid=(4,),
            in_specs=[
                pl.BlockSpec((2, 256, 128), lambda s, t: (s, 0, 0)),
                WHOLE,
                WHOLE,
                pl.BlockSpec((2, 2, 80, 256), lambda s, t: (s, 0, 0, 0)),
                pl.BlockSpec((2, 2, 8, 256), lambda s, t: (s, 0, 0, 0)),
            ],
            out_specs=pl.BlockSpec((8, 128, 256), lambda s, t: (0, 0, 0)),
            scratch_shapes=[pltpu.VMEM((2, 1536, 256), F32), pltpu.VMEM((2, 1536, 256), BF16)],
        ),
        out_shape=jax.ShapeDtypeStruct((8, 128, 256), BF16),
        name="attend",
    )(table, queries, on_chip(low), on_chip(high), own_total, own_top)


def output_kernel(table, mixed_ref, mine_ref, other_ref, voxels_ref, out_ref):
    rows = [r * 128 + y * 16 for y in range(8) for r in range(8)]
    mixed = jnp.concatenate([mixed_ref[row : row + 16, :] for row in rows], axis=0).T
    for pair in range(4):
        ref = (mine_ref, other_ref)[pair // 2]
        slots = (2 * pair, 2 * pair + 1)
        weight = jnp.concatenate([ref[slot % 4] for slot in slots], axis=1)
        projected = jnp.dot(mixed, weight, preferred_element_type=F32)
        for place, slot in enumerate(slots):
            start = pl.multiple_of(region_of(slot, table[72], table[73]) * 128, 128)
            cols = pl.ds(start, 128)
            part = projected[:, place * 128 : place * 128 + 128]
            out_ref[:, cols] = (voxels_ref[:, cols].astype(F32) + part).astype(BF16)


def project_out(table, mixed, mine, other, voxels):
    return pl.pallas_call(
        output_kernel,
        grid_spec=pltpu.PrefetchScalarGridSpec(
            num_scalar_prefetch=1,
            grid=(1,),
            in_specs=[
                pl.BlockSpec(memory_space=pltpu.VMEM),
                pl.BlockSpec((4, 1024, 128), lambda n, t: (0, 0, 0)),
                pl.BlockSpec((4, 1024, 128), lambda n, t: (0, 0, 0)),
                pl.BlockSpec((256, 1024), lambda n, t: (0, 0)),
            ],
            out_specs=pl.BlockSpec((256, 1024), lambda n, t: (0, 0)),
        ),
        out_shape=jax.ShapeDtypeStruct((256, 1024), BF16),
        name="project_out",
    )(table, on_chip(mixed), mine, other, voxels)


def gathered_line(value):
    pieces = [value]
    for step in (1, -1, 2):
        pieces.append(shift(value, "x", step))
    mine = jnp.concatenate(pieces, axis=0)
    return (mine, shift(mine, "c", 1))


def layer(voxels, norm_gain, qkv_weight, out_weight, neighbours):
    x, c, y, z = (lax.axis_index(a) for a in ("x", "c", "y", "z"))
    region, owner = (2 * x + c, 8 * y + z)
    tokens = voxels.reshape(256, 1024)
    ids = neighbours.reshape(1, 8)
    entry = jnp.arange(128, dtype=jnp.int32)[:, None]
    near_region = region + entry // 3 - 1
    near_owner = owner + entry % 3 - 1
    inside = (
        (entry < 9) & (near_region >= 0) & (near_region < 8) & (near_owner >= 0) & (near_owner < 64)
    )
    listed = jnp.any((ids == near_region * 64 + near_owner) & inside, axis=1) | (entry[:, 0] == 4)

    normed = layer_norm(tokens, norm_gain)
    mine, other = gathered_line(normed)

    parts = qkv_weight.reshape(2, 3, 8, 128)
    flags = jnp.broadcast_to(listed.astype(BF16)[None, None], (2, 8, 128))
    parts = [parts[:, 1], parts[:, 2], parts[:, 0], out_weight.reshape(2, 8, 128), flags]
    parts = jnp.stack(parts, axis=2).transpose(1, 0, 2, 3).reshape(8, 1, 2, 640)
    parts = jnp.broadcast_to(parts, (8, 8, 2, 640)).reshape(64, 2, 640)
    swapped = lax.all_to_all(parts, ("x", "c", "z"), 0, 0, tiled=True)
    masks = lax.dynamic_index_in_dim(swapped.reshape(8, 8, 2, 640), z, 1, keepdims=False)
    table = jnp.concatenate([
        masks[:, 0, 512:521].astype(jnp.int32).reshape(72),
        jnp.stack([x, c]).astype(jnp.int32),
    ])
    swapped = swapped.reshape(128, 640)

    weight = from_everyone(swapped[:, :384], "y")
    own, queries = project_qkv(mine, other, weight)
    line = [(i, i + 1) for i in range(63)]
    low = lax.ppermute(own, PLANE, line)
    high = lax.ppermute(own, PLANE, [(j, i) for i, j in line])

    out_part, _ = lax.optimization_barrier((swapped[:, 384:512], queries))
    out_part = from_everyone(out_part, "y").reshape(1024, 128)
    own_total, own_top = attend_own(table, queries, own)
    out_mine, out_other = gathered_line(out_part)
    mixed = attend(table, queries, low, high, own_total, own_top)
    mixed = lax.all_to_all(mixed, LINE, 0, 0, tiled=True).reshape(1024, 256)
    out_mine, out_other = (part.reshape(4, 1024, 128) for part in (out_mine, out_other))
    result = project_out(table, mixed, out_mine, out_other, tokens)
    return result.reshape(voxels.shape)


def solution(mesh):
    fine = Mesh(mesh.devices.reshape(4, 2, 8, 8), ("x", "c", "y", "z"))
    return jax.shard_map(
        layer,
        mesh=fine,
        in_specs=(
            P(LINE, PLANE, None, None, None),
            P(),
            P((*LINE, *PLANE), None),
            P((*LINE, *PLANE), None),
            P(LINE, PLANE, None, None),
        ),
        out_specs=P(LINE, PLANE, None, None, None),
        check_vma=False,
    )
```

```python
import functools

import jax
import jax.numpy as jnp
from jax import lax
from jax.experimental import pallas as pl
from jax.experimental.pallas import tpu as pltpu
from jax.sharding import Mesh, PartitionSpec as P


HEAD_DIM = 64
FACTOR = HEAD_DIM ** (-0.5) * 1.4426950408889634
LINE = ("x", "c")
PLANE = ("y", "z")
BF16 = jnp.bfloat16
F32 = jnp.float32


def norm_kernel(tokens_ref, gain_ref, out_ref):
    widened = tokens_ref[...].astype(F32)
    average = jnp.mean(widened, axis=-1, keepdims=True)
    centred = widened - average
    spread = jnp.mean(centred * centred, axis=-1, keepdims=True)
    out_ref[...] = (centred * lax.rsqrt(spread + 1e-06) * gain_ref[...]).astype(BF16)


def layer_norm(tokens, norm_gain):
    return pl.pallas_call(
        norm_kernel,
        grid=(2,),
        in_specs=[
            pl.BlockSpec((128, 1024), lambda i: (i, 0)),
            pl.BlockSpec((1, 1024), lambda i: (0, 0)),
        ],
        out_specs=pl.BlockSpec((128, 1024), lambda i: (i, 0)),
        out_shape=jax.ShapeDtypeStruct((256, 1024), BF16),
        name="layer_norm",
    )(tokens, norm_gain.reshape(1, 1024))


def message_kernel(lists_ref, weight_ref, out_weight_ref, out_ref):
    region = 2 * lax.axis_index("x") + lax.axis_index("c")
    owner = 8 * lax.axis_index("y") + lax.axis_index("z")
    lanes = lax.broadcasted_iota(jnp.int32, (2, 128), 1)
    flags = jnp.where(lanes == 4, 1.0, 0.0)
    for entry in (0, 1, 2, 3, 5, 6, 7, 8):
        near_region = region + entry // 3 - 1
        near_owner = owner + entry % 3 - 1
        inside = (
            (near_region >= 0) & (near_region < 8) & (near_owner >= 0) & (near_owner < 64)
        )
        number = jnp.where(inside, near_region * 64 + near_owner, -2)
        listed = functools.reduce(jnp.logical_or, [lists_ref[0, i] == number for i in range(8)])
        flags = jnp.where((lanes == entry) & listed, 1.0, flags)
    flags = flags.astype(BF16)
    for head_pair in range(8):
        start = head_pair * 128
        parts = [weight_ref[:, base + start : base + start + 128] for base in (1024, 2048, 0)]
        parts += [out_weight_ref[:, start : start + 128], flags]
        message = jnp.concatenate(parts, axis=1)
        for z in range(8):
            out_ref[head_pair * 8 + z] = message


def messages(lists, weight, out_weight):
    return pl.pallas_call(
        message_kernel,
        in_specs=[
            pl.BlockSpec(memory_space=pltpu.SMEM),
            pl.BlockSpec(memory_space=pltpu.VMEM),
            pl.BlockSpec(memory_space=pltpu.VMEM),
        ],
        out_shape=jax.ShapeDtypeStruct((64, 2, 640), BF16),
        name="messages",
    )(lists, weight, out_weight)


def shift(value, axis, step):
    n = lax.axis_size(axis)
    return lax.ppermute(value, axis, [(i, (i + step) % n) for i in range(n)])


def from_everyone(value, axes):
    n = lax.axis_size(axes)
    return lax.all_to_all(jnp.broadcast_to(value[None], (n, *value.shape)), axes, 0, 0, tiled=True)


def region_of(slot, x, c):
    parity, place = (slot // 4, slot % 4)
    step = jnp.where(place == 0, 0, jnp.where(place == 1, 3, place - 1))
    return 2 * ((x + step) % 4) + (c + parity) % 2


def slot_of(region, x, c):
    step = (region // 2 - x + 4) % 4
    place = jnp.where(step == 0, 0, jnp.where(step == 3, 1, step + 1))
    return 4 * ((region % 2 + c) % 2) + place


WHOLE = pl.BlockSpec(memory_space=pltpu.VMEM)


def on_chip(value):
    return pltpu.with_memory_space_constraint(value, pltpu.VMEM)


def project_tokens(tokens, weight, kv_ref, query_ref):
    projected = jnp.dot(tokens, weight, preferred_element_type=F32)
    for block in range(2):
        rows = slice(block * 256, block * 256 + 256)
        kv_ref[block, 0:256, :] = projected[rows, :128].astype(BF16)
        values = projected[rows, 128:256].astype(BF16).T
        kv_ref[block, 256:384, :] = values[:, :128]
        kv_ref[block, 384:512, :] = values[:, 128:]
        query_ref[block] = (projected[rows, 256:] * FACTOR).astype(BF16)


def mine_kernel(tokens_ref, gathered_ref, kv_ref, query_ref, weight_ref):
    @pl.when(pl.program_id(0) == 0)
    def _():
        for region in range(8):
            for y in range(8):
                row = region * 128 + y * 16
                weight_ref[row : row + 16] = gathered_ref[y, region * 16 : region * 16 + 16]

    project_tokens(tokens_ref[...], weight_ref[...], kv_ref, query_ref)


def other_kernel(tokens_ref, weight_ref, _, __, kv_ref, query_ref):
    rows = pl.ds(pl.multiple_of(pl.program_id(0) * 512, 512), 512)
    project_tokens(tokens_ref[rows, :], weight_ref[...], kv_ref, query_ref)


def project_call(kernel, first, weight_out, aliased):
    whole = pl.BlockSpec((1024, 384), lambda s: (0, 0))
    on_chip_spec = pl.BlockSpec(memory_space=pltpu.VMEM)
    return pl.pallas_call(
        kernel,
        grid=(2,),
        in_specs=[
            pl.BlockSpec((512, 1024), lambda s: (s, 0)) if weight_out else on_chip_spec,
            on_chip_spec if weight_out else whole,
            *[pl.BlockSpec(memory_space=pl.ANY)] * aliased,
        ],
        out_specs=[
            pl.BlockSpec((2, 512, 128), lambda s: (2 * first + s, 0, 0)),
            pl.BlockSpec((2, 256, 128), lambda s: (2 * first + s, 0, 0)),
            *[whole] * weight_out,
        ],
        out_shape=[
            jax.ShapeDtypeStruct((8, 512, 128), BF16),
            jax.ShapeDtypeStruct((8, 256, 128), BF16),
            *[jax.ShapeDtypeStruct((1024, 384), BF16)] * weight_out,
        ],
        input_output_aliases={2: 0, 3: 1} if aliased else {},
    )


def near_places(table, slot, refs):
    x, c = (table[72], table[73])
    region = region_of(slot, x, c)
    places = []
    for side, ref in refs:
        for step in range(3):
            near = jnp.clip(region + step - 1, 0, 7)
            flag = table[region * 9 + step * 3 + side]
            places.append((ref, slot_of(near, x, c), jnp.where(flag > 0, 0.0, 1e30).astype(F32)))
    return places


def run_units(table, query_ref, refs, score_ref, weight_ref, known_top, finish):
    lanes = lax.broadcasted_iota(jnp.int32, (256, 128), 1)
    units = []
    for place in range(2):
        places = near_places(table, pl.program_id(0) * 2 + place, refs)
        for head in range(2):
            inside = (lanes >= head * 64) & (lanes < head * 64 + 64)
            query = jnp.where(inside, query_ref[place], jnp.zeros((), BF16))
            units.append((place, head, places, query))
    count = len(units[0][2])
    ones = jnp.ones((16, count * 256), BF16)
    tops = []
    for turn in range(5):
        column_tops = []
        for entry in range(count):
            rows = slice(entry * 256, entry * 256 + 256)
            if turn < 4:
                _, _, places, query = units[turn]
                ref, slot, penalty = places[entry]
                scores = lax.dot_general(
                    ref[slot, 0:256, :], query, (((1,), (1,)), ((), ())),
                    preferred_element_type=F32,
                )
                score_ref[turn % 2, rows] = scores
                column_tops.append(jnp.max(scores, axis=0, keepdims=True) - penalty)
            if turn > 0:
                penalty = units[turn - 1][2][entry][2]
                weight_ref[(turn - 1) % 2, rows] = jnp.exp2(
                    score_ref[(turn - 1) % 2, rows] - (tops[-1] + penalty)
                ).astype(BF16)
        if turn > 0:
            place, head, places, _ = units[turn - 1]
            halves = []
            for ref, slot, _ in places:
                halves.append(ref[slot, 256 + head * 64 : 320 + head * 64, :])
                halves.append(ref[slot, 384 + head * 64 : 448 + head * 64, :])
            values = jnp.concatenate([jnp.concatenate(halves, axis=1), ones], axis=0)
            total = jnp.dot(values, weight_ref[(turn - 1) % 2], preferred_element_type=F32)
            finish(place, head, tops[-1], total)
        if turn < 4:
            top = functools.reduce(jnp.maximum, column_tops)
            if known_top is not None:
                top = jnp.maximum(top, known_top(*units[turn][:2]))
            tops.append(top)


def attend_own_kernel(
    table, query_ref, own_ref, total_ref, top_ref, score_ref, weight_ref
):
    def finish(place, head, top, total):
        total_ref[place, head] = total
        top_ref[place, head] = jnp.broadcast_to(top, (8, 256))

    run_units(table, query_ref, [(1, own_ref)], score_ref, weight_ref, None, finish)


def attend_own(table, queries, own):
    return pl.pallas_call(
        attend_own_kernel,
        grid_spec=pltpu.PrefetchScalarGridSpec(
            num_scalar_prefetch=1,
            grid=(4,),
            in_specs=[pl.BlockSpec((2, 256, 128), lambda s, t: (s, 0, 0)), WHOLE],
            out_specs=[
                pl.BlockSpec((2, 2, 80, 256), lambda s, t: (s, 0, 0, 0)),
                pl.BlockSpec((2, 2, 8, 256), lambda s, t: (s, 0, 0, 0)),
            ],
            scratch_shapes=[pltpu.VMEM((2, 768, 256), F32), pltpu.VMEM((2, 768, 256), BF16)],
        ),
        out_shape=[
            jax.ShapeDtypeStruct((8, 2, 80, 256), F32),
            jax.ShapeDtypeStruct((8, 2, 8, 256), F32),
        ],
        name="attend_own",
    )(table, queries, own)


def attend_kernel(
    table, query_ref, low_ref, high_ref, own_total_ref, own_top_ref, out_ref, score_ref, weight_ref
):
    def known_top(place, head):
        return own_top_ref[place, head, 0:1]

    def finish(place, head, top, total):
        total += own_total_ref[place, head] * jnp.exp2(known_top(place, head) - top)
        region = region_of(pl.program_id(0) * 2 + place, table[72], table[73])
        out_ref[region, head * 64 : head * 64 + 64, :] = (total[:64] / total[64:65]).astype(BF16)

    run_units(table, query_ref, [(0, low_ref), (2, high_ref)], score_ref, weight_ref, known_top, finish)


def attend(table, queries, low, high, own_total, own_top):
    return pl.pallas_call(
        attend_kernel,
        grid_spec=pltpu.PrefetchScalarGridSpec(
            num_scalar_prefetch=1,
            grid=(4,),
            in_specs=[
                pl.BlockSpec((2, 256, 128), lambda s, t: (s, 0, 0)),
                WHOLE,
                WHOLE,
                pl.BlockSpec((2, 2, 80, 256), lambda s, t: (s, 0, 0, 0)),
                pl.BlockSpec((2, 2, 8, 256), lambda s, t: (s, 0, 0, 0)),
            ],
            out_specs=pl.BlockSpec((8, 128, 256), lambda s, t: (0, 0, 0)),
            scratch_shapes=[pltpu.VMEM((2, 1536, 256), F32), pltpu.VMEM((2, 1536, 256), BF16)],
        ),
        out_shape=jax.ShapeDtypeStruct((8, 128, 256), BF16),
        name="attend",
    )(table, queries, on_chip(low), on_chip(high), own_total, own_top)


def output_kernel(table, mixed_ref, mine_ref, other_ref, voxels_ref, out_ref, turned_ref):
    @pl.when(pl.program_id(0) == 0)
    def _():
        rows = [r * 128 + y * 16 for y in range(8) for r in range(8)]
        mixed = jnp.concatenate([mixed_ref[row : row + 16, :] for row in rows], axis=0)
        turned_ref[...] = mixed.T

    weight = jnp.concatenate([mine_ref[0], other_ref[0]], axis=1)
    projected = jnp.dot(turned_ref[...], weight, preferred_element_type=F32)
    c = table[73]
    for place, parity in enumerate((c, 1 - c)):
        cols = pl.ds(pl.multiple_of(parity * 128, 128), 128)
        part = projected[:, place * 128 : place * 128 + 128]
        out_ref[:, cols] = (voxels_ref[:, cols].astype(F32) + part).astype(BF16)


def project_out(table, mixed, mine, other, voxels):
    return pl.pallas_call(
        output_kernel,
        grid_spec=pltpu.PrefetchScalarGridSpec(
            num_scalar_prefetch=1,
            grid=(4,),
            in_specs=[
                pl.BlockSpec(memory_space=pltpu.VMEM),
                pl.BlockSpec((1, 1024, 128), lambda n, t: (n, 0, 0)),
                pl.BlockSpec((1, 1024, 128), lambda n, t: (n, 0, 0)),
                pl.BlockSpec((256, 256), lambda n, t: (0, n)),
            ],
            out_specs=pl.BlockSpec((256, 256), lambda n, t: (0, n)),
            scratch_shapes=[pltpu.VMEM((256, 1024), BF16)],
        ),
        out_shape=jax.ShapeDtypeStruct((256, 1024), BF16),
        name="project_out",
    )(table, on_chip(mixed), mine, other, voxels)


def gathered_line(value):
    pieces = [value]
    for step in (1, -1, 2):
        pieces.append(shift(value, "x", step))
    mine = jnp.concatenate(pieces, axis=0)
    return (mine, shift(mine, "c", 1))


def layer(voxels, norm_gain, qkv_weight, out_weight, neighbours):
    x, c, z = (lax.axis_index(a) for a in ("x", "c", "z"))
    tokens = voxels.reshape(256, 1024)
    normed = layer_norm(tokens, norm_gain)
    mine, other = gathered_line(normed)

    parts = messages(neighbours.reshape(1, 8), qkv_weight, out_weight)
    swapped = lax.all_to_all(parts, ("x", "c", "z"), 0, 0, tiled=True)
    masks = lax.dynamic_index_in_dim(swapped.reshape(8, 8, 2, 640), z, 1, keepdims=False)
    table = jnp.concatenate([
        masks[:, 0, 512:521].astype(jnp.int32).reshape(72),
        jnp.stack([x, c]).astype(jnp.int32),
    ])
    swapped = swapped.reshape(128, 640)

    weight = from_everyone(swapped[:, :384], "y")
    own, queries, weight = project_call(mine_kernel, 0, 1, 0)(mine, on_chip(weight))
    own, queries = project_call(other_kernel, 1, 0, 2)(on_chip(other), weight, own, queries)
    line = [(i, i + 1) for i in range(63)]
    low = lax.ppermute(own, PLANE, line)
    high = lax.ppermute(own, PLANE, [(j, i) for i, j in line])

    out_part, _ = lax.optimization_barrier((swapped[:, 384:512], queries))
    out_part = from_everyone(out_part, "y").reshape(1024, 128)
    own_total, own_top = attend_own(table, queries, own)
    out_mine = from_everyone(out_part, "x")
    out_other = shift(out_mine, "c", 1)
    mixed = attend(table, queries, low, high, own_total, own_top)
    mixed = lax.all_to_all(mixed, LINE, 0, 0, tiled=True).reshape(1024, 256)
    result = project_out(table, mixed, out_mine, out_other, tokens)
    return result.reshape(voxels.shape)


def solution(mesh):
    fine = Mesh(mesh.devices.reshape(4, 2, 8, 8), ("x", "c", "y", "z"))
    return jax.shard_map(
        layer,
        mesh=fine,
        in_specs=(
            P(LINE, PLANE, None, None, None),
            P(),
            P((*LINE, *PLANE), None),
            P((*LINE, *PLANE), None),
            P(LINE, PLANE, None, None),
        ),
        out_specs=P(LINE, PLANE, None, None, None),
        check_vma=False,
    )
```

```python
import functools

import jax
import jax.numpy as jnp
from jax import lax
from jax.experimental import pallas as pl
from jax.experimental.pallas import tpu as pltpu
from jax.sharding import Mesh, PartitionSpec as P


HEAD_DIM = 64
FACTOR = HEAD_DIM ** (-0.5) * 1.4426950408889634
LINE = ("x", "c")
PLANE = ("y", "z")
BF16 = jnp.bfloat16
F32 = jnp.float32


def norm_kernel(tokens_ref, gain_ref, out_ref):
    widened = tokens_ref[...].astype(F32)
    average = jnp.mean(widened, axis=-1, keepdims=True)
    centred = widened - average
    spread = jnp.mean(centred * centred, axis=-1, keepdims=True)
    out_ref[...] = (centred * lax.rsqrt(spread + 1e-06) * gain_ref[...]).astype(BF16)


def layer_norm(tokens, norm_gain):
    return pl.pallas_call(
        norm_kernel,
        grid=(2,),
        in_specs=[
            pl.BlockSpec((128, 1024), lambda i: (i, 0)),
            pl.BlockSpec((1, 1024), lambda i: (0, 0)),
        ],
        out_specs=pl.BlockSpec((128, 1024), lambda i: (i, 0)),
        out_shape=jax.ShapeDtypeStruct((256, 1024), BF16),
        name="layer_norm",
    )(tokens, norm_gain.reshape(1, 1024))


def message_kernel(lists_ref, weight_ref, out_weight_ref, out_ref):
    region = 2 * lax.axis_index("x") + lax.axis_index("c")
    owner = 8 * lax.axis_index("y") + lax.axis_index("z")
    lanes = lax.broadcasted_iota(jnp.int32, (2, 128), 1)
    flags = jnp.where(lanes == 4, 1.0, 0.0)
    for entry in (0, 1, 2, 3, 5, 6, 7, 8):
        near_region = region + entry // 3 - 1
        near_owner = owner + entry % 3 - 1
        inside = (
            (near_region >= 0) & (near_region < 8) & (near_owner >= 0) & (near_owner < 64)
        )
        number = jnp.where(inside, near_region * 64 + near_owner, -2)
        listed = functools.reduce(jnp.logical_or, [lists_ref[0, i] == number for i in range(8)])
        flags = jnp.where((lanes == entry) & listed, 1.0, flags)
    flags = flags.astype(BF16)
    for head_pair in range(8):
        start = head_pair * 128
        parts = [weight_ref[:, base + start : base + start + 128] for base in (1024, 2048, 0)]
        parts += [out_weight_ref[:, start : start + 128], flags]
        message = jnp.concatenate(parts, axis=1)
        for z in range(8):
            out_ref[head_pair * 8 + z] = message


def messages(lists, weight, out_weight):
    return pl.pallas_call(
        message_kernel,
        in_specs=[
            pl.BlockSpec(memory_space=pltpu.SMEM),
            pl.BlockSpec(memory_space=pltpu.VMEM),
            pl.BlockSpec(memory_space=pltpu.VMEM),
        ],
        out_shape=jax.ShapeDtypeStruct((64, 2, 640), BF16),
        name="messages",
    )(lists, weight, out_weight)


def shift(value, axis, step):
    n = lax.axis_size(axis)
    return lax.ppermute(value, axis, [(i, (i + step) % n) for i in range(n)])


def from_everyone(value, axes):
    n = lax.axis_size(axes)
    return lax.all_to_all(jnp.broadcast_to(value[None], (n, *value.shape)), axes, 0, 0, tiled=True)


def region_of(slot, x, c):
    parity, place = (slot // 4, slot % 4)
    step = jnp.where(place == 0, 0, jnp.where(place == 1, 3, place - 1))
    return 2 * ((x + step) % 4) + (c + parity) % 2


def slot_of(region, x, c):
    step = (region // 2 - x + 4) % 4
    place = jnp.where(step == 0, 0, jnp.where(step == 3, 1, step + 1))
    return 4 * ((region % 2 + c) % 2) + place


WHOLE = pl.BlockSpec(memory_space=pltpu.VMEM)


def on_chip(value):
    return pltpu.with_memory_space_constraint(value, pltpu.VMEM)


def qkv_kernel(mine_ref, other_ref, gathered_ref, kv_ref, query_ref, weight_ref):
    @pl.when(pl.program_id(0) == 0)
    def _():
        for region in range(8):
            for y in range(8):
                row = region * 128 + y * 16
                weight_ref[row : row + 16] = gathered_ref[y, region * 16 : region * 16 + 16]

    def project(tokens):
        projected = jnp.dot(tokens, weight_ref[...], preferred_element_type=F32)
        for block in range(2):
            rows = slice(block * 256, block * 256 + 256)
            kv_ref[block, 0:256, :] = projected[rows, :128].astype(BF16)
            values = projected[rows, 128:256].astype(BF16).T
            kv_ref[block, 256:384, :] = values[:, :128]
            kv_ref[block, 384:512, :] = values[:, 128:]
            query_ref[block] = (projected[rows, 256:] * FACTOR).astype(BF16)

    @pl.when(pl.program_id(0) < 2)
    def _():
        project(mine_ref[...])

    @pl.when(pl.program_id(0) >= 2)
    def _():
        project(other_ref[...])


def project_qkv(mine, other, weight):
    return pl.pallas_call(
        qkv_kernel,
        grid=(4,),
        in_specs=[
            pl.BlockSpec((512, 1024), lambda s: (jnp.minimum(s, 1), 0)),
            pl.BlockSpec((512, 1024), lambda s: (jnp.maximum(s - 2, 0), 0)),
            pl.BlockSpec(memory_space=pltpu.VMEM),
        ],
        out_specs=[
            pl.BlockSpec((2, 512, 128), lambda s: (s, 0, 0)),
            pl.BlockSpec((2, 256, 128), lambda s: (s, 0, 0)),
        ],
        out_shape=[
            jax.ShapeDtypeStruct((8, 512, 128), BF16),
            jax.ShapeDtypeStruct((8, 256, 128), BF16),
        ],
        scratch_shapes=[pltpu.VMEM((1024, 384), BF16)],
        name="project_qkv",
    )(mine, other, on_chip(weight))


def near_places(table, slot, refs):
    x, c = (table[72], table[73])
    region = region_of(slot, x, c)
    places = []
    for side, ref in refs:
        for step in range(3):
            near = jnp.clip(region + step - 1, 0, 7)
            flag = table[region * 9 + step * 3 + side]
            places.append((ref, slot_of(near, x, c), jnp.where(flag > 0, 0.0, 1e30).astype(F32)))
    return places


def run_units(table, query_ref, refs, score_ref, weight_ref, known_top, finish):
    lanes = lax.broadcasted_iota(jnp.int32, (256, 128), 1)
    units = []
    for place in range(2):
        places = near_places(table, pl.program_id(0) * 2 + place, refs)
        for head in range(2):
            inside = (lanes >= head * 64) & (lanes < head * 64 + 64)
            query = jnp.where(inside, query_ref[place], jnp.zeros((), BF16))
            units.append((place, head, places, query))
    count = len(units[0][2])
    ones = jnp.ones((16, count * 256), BF16)
    tops = []
    for turn in range(5):
        column_tops = []
        for entry in range(count):
            rows = slice(entry * 256, entry * 256 + 256)
            if turn < 4:
                _, _, places, query = units[turn]
                ref, slot, penalty = places[entry]
                scores = lax.dot_general(
                    ref[slot, 0:256, :], query, (((1,), (1,)), ((), ())),
                    preferred_element_type=F32,
                )
                score_ref[turn % 2, rows] = scores
                column_tops.append(jnp.max(scores, axis=0, keepdims=True) - penalty)
            if turn > 0:
                penalty = units[turn - 1][2][entry][2]
                weight_ref[(turn - 1) % 2, rows] = jnp.exp2(
                    score_ref[(turn - 1) % 2, rows] - (tops[-1] + penalty)
                ).astype(BF16)
        if turn > 0:
            place, head, places, _ = units[turn - 1]
            halves = []
            for ref, slot, _ in places:
                halves.append(ref[slot, 256 + head * 64 : 320 + head * 64, :])
                halves.append(ref[slot, 384 + head * 64 : 448 + head * 64, :])
            values = jnp.concatenate([jnp.concatenate(halves, axis=1), ones], axis=0)
            total = jnp.dot(values, weight_ref[(turn - 1) % 2], preferred_element_type=F32)
            finish(place, head, tops[-1], total)
        if turn < 4:
            top = functools.reduce(jnp.maximum, column_tops)
            if known_top is not None:
                top = jnp.maximum(top, known_top(*units[turn][:2]))
            tops.append(top)


def attend_own_kernel(
    table, query_ref, own_ref, total_ref, top_ref, score_ref, weight_ref
):
    def finish(place, head, top, total):
        total_ref[place, head] = total
        top_ref[place, head] = jnp.broadcast_to(top, (8, 256))

    run_units(table, query_ref, [(1, own_ref)], score_ref, weight_ref, None, finish)


def attend_own(table, queries, own):
    return pl.pallas_call(
        attend_own_kernel,
        grid_spec=pltpu.PrefetchScalarGridSpec(
            num_scalar_prefetch=1,
            grid=(4,),
            in_specs=[pl.BlockSpec((2, 256, 128), lambda s, t: (s, 0, 0)), WHOLE],
            out_specs=[
                pl.BlockSpec((2, 2, 80, 256), lambda s, t: (s, 0, 0, 0)),
                pl.BlockSpec((2, 2, 8, 256), lambda s, t: (s, 0, 0, 0)),
            ],
            scratch_shapes=[pltpu.VMEM((2, 768, 256), F32), pltpu.VMEM((2, 768, 256), BF16)],
        ),
        out_shape=[
            jax.ShapeDtypeStruct((8, 2, 80, 256), F32),
            jax.ShapeDtypeStruct((8, 2, 8, 256), F32),
        ],
        name="attend_own",
    )(table, queries, own)


def attend_kernel(
    table, query_ref, low_ref, high_ref, own_total_ref, own_top_ref, out_ref, score_ref, weight_ref
):
    def known_top(place, head):
        return own_top_ref[place, head, 0:1]

    def finish(place, head, top, total):
        total += own_total_ref[place, head] * jnp.exp2(known_top(place, head) - top)
        region = region_of(pl.program_id(0) * 2 + place, table[72], table[73])
        out_ref[region, head * 64 : head * 64 + 64, :] = (total[:64] / total[64:65]).astype(BF16)

    run_units(table, query_ref, [(0, low_ref), (2, high_ref)], score_ref, weight_ref, known_top, finish)


def attend(table, queries, low, high, own_total, own_top):
    return pl.pallas_call(
        attend_kernel,
        grid_spec=pltpu.PrefetchScalarGridSpec(
            num_scalar_prefetch=1,
            grid=(4,),
            in_specs=[
                pl.BlockSpec((2, 256, 128), lambda s, t: (s, 0, 0)),
                WHOLE,
                WHOLE,
                pl.BlockSpec((2, 2, 80, 256), lambda s, t: (s, 0, 0, 0)),
                pl.BlockSpec((2, 2, 8, 256), lambda s, t: (s, 0, 0, 0)),
            ],
            out_specs=pl.BlockSpec((8, 128, 256), lambda s, t: (0, 0, 0)),
            scratch_shapes=[pltpu.VMEM((2, 1536, 256), F32), pltpu.VMEM((2, 1536, 256), BF16)],
        ),
        out_shape=jax.ShapeDtypeStruct((8, 128, 256), BF16),
        name="attend",
    )(table, queries, on_chip(low), on_chip(high), own_total, own_top)


def output_kernel(table, mixed_ref, mine_ref, other_ref, voxels_ref, out_ref, turned_ref):
    @pl.when(pl.program_id(0) == 0)
    def _():
        rows = [r * 128 + y * 16 for y in range(8) for r in range(8)]
        mixed = jnp.concatenate([mixed_ref[row : row + 16, :] for row in rows], axis=0)
        turned_ref[...] = mixed.T

    weight = jnp.concatenate([mine_ref[0], other_ref[pl.program_id(0)]], axis=1)
    projected = jnp.dot(turned_ref[...], weight, preferred_element_type=F32)
    c = table[73]
    for place, parity in enumerate((c, 1 - c)):
        cols = pl.ds(pl.multiple_of(parity * 128, 128), 128)
        part = projected[:, place * 128 : place * 128 + 128]
        out_ref[:, cols] = (voxels_ref[:, cols].astype(F32) + part).astype(BF16)


def project_out(table, mixed, mine, other, voxels):
    return pl.pallas_call(
        output_kernel,
        grid_spec=pltpu.PrefetchScalarGridSpec(
            num_scalar_prefetch=1,
            grid=(4,),
            in_specs=[
                pl.BlockSpec(memory_space=pltpu.VMEM),
                pl.BlockSpec((1, 1024, 128), lambda n, t: (n, 0, 0)),
                pl.BlockSpec(memory_space=pltpu.VMEM),
                pl.BlockSpec((256, 256), lambda n, t: (0, n)),
            ],
            out_specs=pl.BlockSpec((256, 256), lambda n, t: (0, n)),
            scratch_shapes=[pltpu.VMEM((256, 1024), BF16)],
        ),
        out_shape=jax.ShapeDtypeStruct((256, 1024), BF16),
        name="project_out",
    )(table, on_chip(mixed), mine, on_chip(other), voxels)


def gathered_line(value):
    pieces = [value]
    for step in (1, -1, 2):
        pieces.append(shift(value, "x", step))
    mine = jnp.concatenate(pieces, axis=0)
    return (mine, shift(mine, "c", 1))


def layer(voxels, norm_gain, qkv_weight, out_weight, neighbours):
    x, c, z = (lax.axis_index(a) for a in ("x", "c", "z"))
    tokens = voxels.reshape(256, 1024)
    normed = layer_norm(tokens, norm_gain)
    mine, other = gathered_line(normed)

    parts = messages(neighbours.reshape(1, 8), qkv_weight, out_weight)
    swapped = lax.all_to_all(parts, ("x", "c", "z"), 0, 0, tiled=True)
    masks = lax.dynamic_index_in_dim(swapped.reshape(8, 8, 2, 640), z, 1, keepdims=False)
    table = jnp.concatenate([
        masks[:, 0, 512:521].astype(jnp.int32).reshape(72),
        jnp.stack([x, c]).astype(jnp.int32),
    ])
    swapped = swapped.reshape(128, 640)

    weight = from_everyone(swapped[:, :384], "y")
    own, queries = project_qkv(mine, other, weight)
    line = [(i, i + 1) for i in range(63)]
    low = lax.ppermute(own, PLANE, line)
    high = lax.ppermute(own, PLANE, [(j, i) for i, j in line])

    out_part, _ = lax.optimization_barrier((swapped[:, 384:512], queries))
    out_part = from_everyone(out_part, "y").reshape(1024, 128)
    own_total, own_top = attend_own(table, queries, own)
    out_mine = from_everyone(out_part, "x")
    out_other = shift(out_mine, "c", 1)
    mixed = attend(table, queries, low, high, own_total, own_top)
    mixed = lax.all_to_all(mixed, LINE, 0, 0, tiled=True).reshape(1024, 256)
    result = project_out(table, mixed, out_mine, out_other, tokens)
    return result.reshape(voxels.shape)


def solution(mesh):
    fine = Mesh(mesh.devices.reshape(4, 2, 8, 8), ("x", "c", "y", "z"))
    return jax.shard_map(
        layer,
        mesh=fine,
        in_specs=(
            P(LINE, PLANE, None, None, None),
            P(),
            P((*LINE, *PLANE), None),
            P((*LINE, *PLANE), None),
            P(LINE, PLANE, None, None),
        ),
        out_specs=P(LINE, PLANE, None, None, None),
        check_vma=False,
    )
```

```python
import functools

import jax
import jax.numpy as jnp
from jax import lax
from jax.experimental import pallas as pl
from jax.experimental.pallas import tpu as pltpu
from jax.sharding import Mesh, PartitionSpec as P


HEAD_DIM = 64
FACTOR = HEAD_DIM ** (-0.5) * 1.4426950408889634
LINE = ("x", "c")
PLANE = ("y", "z")
BF16 = jnp.bfloat16
F32 = jnp.float32


def norm(tokens_ref, gain_ref, out_ref):
    widened = tokens_ref[...].astype(F32)
    average = jnp.mean(widened, axis=-1, keepdims=True)
    centred = widened - average
    spread = jnp.mean(centred * centred, axis=-1, keepdims=True)
    out_ref[...] = (centred * lax.rsqrt(spread + 1e-06) * gain_ref[...]).astype(BF16)


def prepare_kernel(
    lists_ref, tokens_ref, gain_ref, weight_ref, out_weight_ref, normed_ref, messages_ref
):
    norm(tokens_ref, gain_ref, normed_ref)

    @pl.when(pl.program_id(0) == 0)
    def _():
        write_messages(lists_ref, weight_ref, out_weight_ref, messages_ref)


def write_messages(lists_ref, weight_ref, out_weight_ref, out_ref):
    region = 2 * lax.axis_index("x") + lax.axis_index("c")
    owner = 8 * lax.axis_index("y") + lax.axis_index("z")
    lanes = lax.broadcasted_iota(jnp.int32, (2, 128), 1)
    flags = jnp.where(lanes == 4, 1.0, 0.0)
    for entry in (0, 1, 2, 3, 5, 6, 7, 8):
        near_region = region + entry // 3 - 1
        near_owner = owner + entry % 3 - 1
        inside = (
            (near_region >= 0) & (near_region < 8) & (near_owner >= 0) & (near_owner < 64)
        )
        number = jnp.where(inside, near_region * 64 + near_owner, -2)
        listed = functools.reduce(jnp.logical_or, [lists_ref[0, i] == number for i in range(8)])
        flags = jnp.where((lanes == entry) & listed, 1.0, flags)
    flags = flags.astype(BF16)
    for head_pair in range(8):
        start = head_pair * 128
        parts = [weight_ref[:, base + start : base + start + 128] for base in (1024, 2048, 0)]
        parts += [out_weight_ref[:, start : start + 128], flags]
        message = jnp.concatenate(parts, axis=1)
        for z in range(8):
            out_ref[head_pair * 8 + z] = message


def prepare(lists, tokens, gain, weight, out_weight):
    return pl.pallas_call(
        prepare_kernel,
        grid=(2,),
        in_specs=[
            pl.BlockSpec(memory_space=pltpu.SMEM),
            pl.BlockSpec((128, 1024), lambda i: (i, 0)),
            pl.BlockSpec((1, 1024), lambda i: (0, 0)),
            pl.BlockSpec((2, 3072), lambda i: (0, 0)),
            pl.BlockSpec((2, 1024), lambda i: (0, 0)),
        ],
        out_specs=[
            pl.BlockSpec((128, 1024), lambda i: (i, 0)),
            pl.BlockSpec((64, 2, 640), lambda i: (0, 0, 0)),
        ],
        out_shape=[
            jax.ShapeDtypeStruct((256, 1024), BF16),
            jax.ShapeDtypeStruct((64, 2, 640), BF16),
        ],
        name="prepare",
    )(lists, tokens, gain, weight, out_weight)


def shift(value, axis, step):
    n = lax.axis_size(axis)
    return lax.ppermute(value, axis, [(i, (i + step) % n) for i in range(n)])


def from_everyone(value, axes):
    n = lax.axis_size(axes)
    return lax.all_to_all(jnp.broadcast_to(value[None], (n, *value.shape)), axes, 0, 0, tiled=True)


def region_of(slot, x, c):
    parity, place = (slot // 4, slot % 4)
    step = jnp.where(place == 0, 0, jnp.where(place == 1, 3, place - 1))
    return 2 * ((x + step) % 4) + (c + parity) % 2


def slot_of(region, x, c):
    step = (region // 2 - x + 4) % 4
    place = jnp.where(step == 0, 0, jnp.where(step == 3, 1, step + 1))
    return 4 * ((region % 2 + c) % 2) + place


WHOLE = pl.BlockSpec(memory_space=pltpu.VMEM)


def on_chip(value):
    return pltpu.with_memory_space_constraint(value, pltpu.VMEM)


def qkv_kernel(mine_ref, other_ref, gathered_ref, kv_ref, query_ref, weight_ref):
    @pl.when(pl.program_id(0) == 0)
    def _():
        for region in range(8):
            for y in range(8):
                row = region * 128 + y * 16
                weight_ref[row : row + 16] = gathered_ref[y, region * 16 : region * 16 + 16]

    def project(tokens):
        projected = jnp.dot(tokens, weight_ref[...], preferred_element_type=F32)
        for block in range(2):
            rows = slice(block * 256, block * 256 + 256)
            kv_ref[block, 0:256, :] = projected[rows, :128].astype(BF16)
            values = projected[rows, 128:256].astype(BF16).T
            kv_ref[block, 256:384, :] = values[:, :128]
            kv_ref[block, 384:512, :] = values[:, 128:]
            query_ref[block] = (projected[rows, 256:] * FACTOR).astype(BF16)

    @pl.when(pl.program_id(0) < 2)
    def _():
        project(mine_ref[...])

    @pl.when(pl.program_id(0) >= 2)
    def _():
        project(other_ref[...])


def project_qkv(mine, other, weight):
    return pl.pallas_call(
        qkv_kernel,
        grid=(4,),
        in_specs=[
            pl.BlockSpec((512, 1024), lambda s: (jnp.minimum(s, 1), 0)),
            pl.BlockSpec((512, 1024), lambda s: (jnp.maximum(s - 2, 0), 0)),
            pl.BlockSpec(memory_space=pltpu.VMEM),
        ],
        out_specs=[
            pl.BlockSpec((2, 512, 128), lambda s: (s, 0, 0)),
            pl.BlockSpec((2, 256, 128), lambda s: (s, 0, 0)),
        ],
        out_shape=[
            jax.ShapeDtypeStruct((8, 512, 128), BF16),
            jax.ShapeDtypeStruct((8, 256, 128), BF16),
        ],
        scratch_shapes=[pltpu.VMEM((1024, 384), BF16)],
        name="project_qkv",
    )(mine, other, on_chip(weight))


def settle_kernel(in_ref, out_ref):
    out_ref[...] = in_ref[...]


def settle(value):
    return pl.pallas_call(
        settle_kernel,
        grid=(4,),
        in_specs=[pl.BlockSpec((256, 1024), lambda i: (i, 0))],
        out_specs=pl.BlockSpec((256, 1024), lambda i: (i, 0)),
        out_shape=jax.ShapeDtypeStruct((1024, 1024), BF16),
        name="settle",
    )(value)


def near_places(table, slot, refs):
    x, c = (table[72], table[73])
    region = region_of(slot, x, c)
    places = []
    for side, ref in refs:
        for step in range(3):
            near = jnp.clip(region + step - 1, 0, 7)
            flag = table[region * 9 + step * 3 + side]
            places.append((ref, slot_of(near, x, c), jnp.where(flag > 0, 0.0, 1e30).astype(F32)))
    return places


def run_units(table, query_ref, refs, score_ref, weight_ref, known_top, finish):
    lanes = lax.broadcasted_iota(jnp.int32, (256, 128), 1)
    units = []
    for place in range(2):
        places = near_places(table, pl.program_id(0) * 2 + place, refs)
        for head in range(2):
            inside = (lanes >= head * 64) & (lanes < head * 64 + 64)
            query = jnp.where(inside, query_ref[place], jnp.zeros((), BF16))
            units.append((place, head, places, query))
    count = len(units[0][2])
    ones = jnp.ones((16, count * 256), BF16)
    tops = []
    for turn in range(5):
        column_tops = []
        for entry in range(count):
            rows = slice(entry * 256, entry * 256 + 256)
            if turn < 4:
                _, _, places, query = units[turn]
                ref, slot, penalty = places[entry]
                scores = lax.dot_general(
                    ref[slot, 0:256, :], query, (((1,), (1,)), ((), ())),
                    preferred_element_type=F32,
                )
                score_ref[turn % 2, rows] = scores
                column_tops.append(jnp.max(scores, axis=0, keepdims=True) - penalty)
            if turn > 0:
                penalty = units[turn - 1][2][entry][2]
                weight_ref[(turn - 1) % 2, rows] = jnp.exp2(
                    score_ref[(turn - 1) % 2, rows] - (tops[-1] + penalty)
                ).astype(BF16)
        if turn > 0:
            place, head, places, _ = units[turn - 1]
            halves = []
            for ref, slot, _ in places:
                halves.append(ref[slot, 256 + head * 64 : 320 + head * 64, :])
                halves.append(ref[slot, 384 + head * 64 : 448 + head * 64, :])
            values = jnp.concatenate([jnp.concatenate(halves, axis=1), ones], axis=0)
            total = jnp.dot(values, weight_ref[(turn - 1) % 2], preferred_element_type=F32)
            finish(place, head, tops[-1], total)
        if turn < 4:
            top = functools.reduce(jnp.maximum, column_tops)
            if known_top is not None:
                top = jnp.maximum(top, known_top(*units[turn][:2]))
            tops.append(top)


def attend_own_kernel(
    table, query_ref, own_ref, total_ref, top_ref, score_ref, weight_ref
):
    def finish(place, head, top, total):
        total_ref[place, head] = total
        top_ref[place, head] = jnp.broadcast_to(top, (8, 256))

    run_units(table, query_ref, [(1, own_ref)], score_ref, weight_ref, None, finish)


def attend_own(table, queries, own):
    return pl.pallas_call(
        attend_own_kernel,
        grid_spec=pltpu.PrefetchScalarGridSpec(
            num_scalar_prefetch=1,
            grid=(4,),
            in_specs=[pl.BlockSpec((2, 256, 128), lambda s, t: (s, 0, 0)), WHOLE],
            out_specs=[
                pl.BlockSpec((2, 2, 80, 256), lambda s, t: (s, 0, 0, 0)),
                pl.BlockSpec((2, 2, 8, 256), lambda s, t: (s, 0, 0, 0)),
            ],
            scratch_shapes=[pltpu.VMEM((2, 768, 256), F32), pltpu.VMEM((2, 768, 256), BF16)],
        ),
        out_shape=[
            jax.ShapeDtypeStruct((8, 2, 80, 256), F32),
            jax.ShapeDtypeStruct((8, 2, 8, 256), F32),
        ],
        name="attend_own",
    )(table, queries, own)


def attend_kernel(
    table, query_ref, low_ref, high_ref, own_total_ref, own_top_ref, out_ref, score_ref, weight_ref
):
    def known_top(place, head):
        return own_top_ref[place, head, 0:1]

    def finish(place, head, top, total):
        total += own_total_ref[place, head] * jnp.exp2(known_top(place, head) - top)
        region = region_of(pl.program_id(0) * 2 + place, table[72], table[73])
        out_ref[region, head * 64 : head * 64 + 64, :] = (total[:64] / total[64:65]).astype(BF16)

    run_units(table, query_ref, [(0, low_ref), (2, high_ref)], score_ref, weight_ref, known_top, finish)


def attend(table, queries, low, high, own_total, own_top):
    return pl.pallas_call(
        attend_kernel,
        grid_spec=pltpu.PrefetchScalarGridSpec(
            num_scalar_prefetch=1,
            grid=(4,),
            in_specs=[
                pl.BlockSpec((2, 256, 128), lambda s, t: (s, 0, 0)),
                WHOLE,
                WHOLE,
                pl.BlockSpec((2, 2, 80, 256), lambda s, t: (s, 0, 0, 0)),
                pl.BlockSpec((2, 2, 8, 256), lambda s, t: (s, 0, 0, 0)),
            ],
            out_specs=pl.BlockSpec((8, 128, 256), lambda s, t: (0, 0, 0)),
            scratch_shapes=[pltpu.VMEM((2, 1536, 256), F32), pltpu.VMEM((2, 1536, 256), BF16)],
        ),
        out_shape=jax.ShapeDtypeStruct((8, 128, 256), BF16),
        name="attend",
    )(table, queries, on_chip(low), on_chip(high), own_total, own_top)


def output_kernel(table, mixed_ref, mine_ref, other_ref, voxels_ref, out_ref):
    rows = [r * 128 + y * 16 for y in range(8) for r in range(8)]
    mixed = jnp.concatenate([mixed_ref[row : row + 16, :] for row in rows], axis=0).T
    c = table[73]
    for chip in range(4):
        weight = jnp.concatenate([mine_ref[chip], other_ref[chip]], axis=1)
        projected = jnp.dot(mixed, weight, preferred_element_type=F32)
        for place, parity in enumerate((c, 1 - c)):
            cols = pl.ds(pl.multiple_of(chip * 256 + parity * 128, 128), 128)
            part = projected[:, place * 128 : place * 128 + 128]
            out_ref[:, cols] = (voxels_ref[:, cols].astype(F32) + part).astype(BF16)


def project_out(table, mixed, mine, other, voxels):
    return pl.pallas_call(
        output_kernel,
        grid_spec=pltpu.PrefetchScalarGridSpec(
            num_scalar_prefetch=1,
            grid=(1,),
            in_specs=[
                pl.BlockSpec(memory_space=pltpu.VMEM),
                pl.BlockSpec((4, 1024, 128), lambda n, t: (0, 0, 0)),
                pl.BlockSpec(memory_space=pltpu.VMEM),
                pl.BlockSpec((256, 1024), lambda n, t: (0, 0)),
            ],
            out_specs=pl.BlockSpec((256, 1024), lambda n, t: (0, 0)),
        ),
        out_shape=jax.ShapeDtypeStruct((256, 1024), BF16),
        name="project_out",
    )(table, on_chip(mixed), mine, on_chip(other), voxels)


def gathered_line(value):
    pieces = [value]
    for step in (1, -1, 2):
        pieces.append(shift(value, "x", step))
    mine = jnp.concatenate(pieces, axis=0)
    return (mine, shift(mine, "c", 1))


def layer(voxels, norm_gain, qkv_weight, out_weight, neighbours):
    x, c, z = (lax.axis_index(a) for a in ("x", "c", "z"))
    tokens = voxels.reshape(256, 1024)
    normed, parts = prepare(
        neighbours.reshape(1, 8), tokens, norm_gain.reshape(1, 1024), qkv_weight, out_weight
    )
    mine, other = gathered_line(normed)
    other = settle(other)

    swapped = lax.all_to_all(parts, ("x", "c", "z"), 0, 0, tiled=True)
    masks = lax.dynamic_index_in_dim(swapped.reshape(8, 8, 2, 640), z, 1, keepdims=False)
    table = jnp.concatenate([
        masks[:, 0, 512:521].astype(jnp.int32).reshape(72),
        jnp.stack([x, c]).astype(jnp.int32),
    ])
    swapped = swapped.reshape(128, 640)

    weight = from_everyone(swapped[:, :384], "y")
    own, queries = project_qkv(mine, other, weight)
    line = [(i, i + 1) for i in range(63)]
    low = lax.ppermute(own, PLANE, line)
    high = lax.ppermute(own, PLANE, [(j, i) for i, j in line])

    out_part, _ = lax.optimization_barrier((swapped[:, 384:512], queries))
    out_part = from_everyone(out_part, "y").reshape(1024, 128)
    own_total, own_top = attend_own(table, queries, own)
    out_mine = from_everyone(out_part, "x")
    out_other = shift(out_mine, "c", 1)
    mixed = attend(table, queries, low, high, own_total, own_top)
    mixed = lax.all_to_all(mixed, LINE, 0, 0, tiled=True).reshape(1024, 256)
    result = project_out(table, mixed, out_mine, out_other, tokens)
    return result.reshape(voxels.shape)


def solution(mesh):
    fine = Mesh(mesh.devices.reshape(4, 2, 8, 8), ("x", "c", "y", "z"))
    return jax.shard_map(
        layer,
        mesh=fine,
        in_specs=(
            P(LINE, PLANE, None, None, None),
            P(),
            P((*LINE, *PLANE), None),
            P((*LINE, *PLANE), None),
            P(LINE, PLANE, None, None),
        ),
        out_specs=P(LINE, PLANE, None, None, None),
        check_vma=False,
    )
```

```python
import functools

import jax
import jax.numpy as jnp
from jax import lax
from jax.experimental import pallas as pl
from jax.experimental.pallas import tpu as pltpu
from jax.sharding import Mesh, PartitionSpec as P


HEAD_DIM = 64
FACTOR = HEAD_DIM ** (-0.5) * 1.4426950408889634
LINE = ("x", "c")
PLANE = ("y", "z")
BF16 = jnp.bfloat16
F32 = jnp.float32


def norm(tokens_ref, gain_ref, out_ref):
    widened = tokens_ref[...].astype(F32)
    average = jnp.mean(widened, axis=-1, keepdims=True)
    centred = widened - average
    spread = jnp.mean(centred * centred, axis=-1, keepdims=True)
    out_ref[...] = (centred * lax.rsqrt(spread + 1e-06) * gain_ref[...]).astype(BF16)


def prepare_kernel(
    lists_ref, tokens_ref, gain_ref, weight_ref, out_weight_ref, normed_ref, messages_ref
):
    norm(tokens_ref, gain_ref, normed_ref)

    @pl.when(pl.program_id(0) == 0)
    def _():
        write_messages(lists_ref, weight_ref, out_weight_ref, messages_ref)


def write_messages(lists_ref, weight_ref, out_weight_ref, out_ref):
    region = 2 * lax.axis_index("x") + lax.axis_index("c")
    owner = 8 * lax.axis_index("y") + lax.axis_index("z")
    lanes = lax.broadcasted_iota(jnp.int32, (2, 128), 1)
    flags = jnp.where(lanes == 4, 1.0, 0.0)
    for entry in (0, 1, 2, 3, 5, 6, 7, 8):
        near_region = region + entry // 3 - 1
        near_owner = owner + entry % 3 - 1
        inside = (
            (near_region >= 0) & (near_region < 8) & (near_owner >= 0) & (near_owner < 64)
        )
        number = jnp.where(inside, near_region * 64 + near_owner, -2)
        listed = functools.reduce(jnp.logical_or, [lists_ref[0, i] == number for i in range(8)])
        flags = jnp.where((lanes == entry) & listed, 1.0, flags)
    flags = flags.astype(BF16)
    for head_pair in range(8):
        start = head_pair * 128
        parts = [weight_ref[:, base + start : base + start + 128] for base in (1024, 2048, 0)]
        parts += [out_weight_ref[:, start : start + 128], flags]
        message = jnp.concatenate(parts, axis=1)
        for z in range(8):
            out_ref[head_pair * 8 + z] = message


def prepare(lists, tokens, gain, weight, out_weight):
    return pl.pallas_call(
        prepare_kernel,
        grid=(2,),
        in_specs=[
            pl.BlockSpec(memory_space=pltpu.SMEM),
            pl.BlockSpec((128, 1024), lambda i: (i, 0)),
            pl.BlockSpec((1, 1024), lambda i: (0, 0)),
            pl.BlockSpec((2, 3072), lambda i: (0, 0)),
            pl.BlockSpec((2, 1024), lambda i: (0, 0)),
        ],
        out_specs=[
            pl.BlockSpec((128, 1024), lambda i: (i, 0)),
            pl.BlockSpec((64, 2, 640), lambda i: (0, 0, 0)),
        ],
        out_shape=[
            jax.ShapeDtypeStruct((256, 1024), BF16),
            jax.ShapeDtypeStruct((64, 2, 640), BF16),
        ],
        name="prepare",
    )(lists, tokens, gain, weight, out_weight)


def shift(value, axis, step):
    n = lax.axis_size(axis)
    return lax.ppermute(value, axis, [(i, (i + step) % n) for i in range(n)])


def from_everyone(value, axes):
    n = lax.axis_size(axes)
    return lax.all_to_all(jnp.broadcast_to(value[None], (n, *value.shape)), axes, 0, 0, tiled=True)


def region_of(slot, x, c):
    parity, place = (slot // 4, slot % 4)
    step = jnp.where(place == 0, 0, jnp.where(place == 1, 3, place - 1))
    return 2 * ((x + step) % 4) + (c + parity) % 2


def slot_of(region, x, c):
    step = (region // 2 - x + 4) % 4
    place = jnp.where(step == 0, 0, jnp.where(step == 3, 1, step + 1))
    return 4 * ((region % 2 + c) % 2) + place


WHOLE = pl.BlockSpec(memory_space=pltpu.VMEM)


def on_chip(value):
    return pltpu.with_memory_space_constraint(value, pltpu.VMEM)


def qkv_kernel(mine_ref, other_ref, gathered_ref, kv_ref, query_ref, weight_ref):
    @pl.when(pl.program_id(0) == 0)
    def _():
        for region in range(8):
            for y in range(8):
                row = region * 128 + y * 16
                weight_ref[row : row + 16] = gathered_ref[y, region * 16 : region * 16 + 16]

    def project(tokens):
        projected = jnp.dot(tokens, weight_ref[...], preferred_element_type=F32)
        for block in range(2):
            rows = slice(block * 256, block * 256 + 256)
            kv_ref[block, 0:256, :] = projected[rows, :128].astype(BF16)
            values = projected[rows, 128:256].astype(BF16).T
            kv_ref[block, 256:384, :] = values[:, :128]
            kv_ref[block, 384:512, :] = values[:, 128:]
            query_ref[block] = (projected[rows, 256:] * FACTOR).astype(BF16)

    @pl.when(pl.program_id(0) < 2)
    def _():
        project(mine_ref[pl.ds(pl.multiple_of(pl.program_id(0) * 512, 512), 512), :])

    @pl.when(pl.program_id(0) >= 2)
    def _():
        project(other_ref[...])


def project_qkv(mine, other, weight):
    return pl.pallas_call(
        qkv_kernel,
        grid=(4,),
        in_specs=[
            pl.BlockSpec(memory_space=pltpu.VMEM),
            pl.BlockSpec((512, 1024), lambda s: (jnp.maximum(s - 2, 0), 0)),
            pl.BlockSpec(memory_space=pltpu.VMEM),
        ],
        out_specs=[
            pl.BlockSpec((2, 512, 128), lambda s: (s, 0, 0)),
            pl.BlockSpec((2, 256, 128), lambda s: (s, 0, 0)),
        ],
        out_shape=[
            jax.ShapeDtypeStruct((8, 512, 128), BF16),
            jax.ShapeDtypeStruct((8, 256, 128), BF16),
        ],
        scratch_shapes=[pltpu.VMEM((1024, 384), BF16)],
        name="project_qkv",
    )(on_chip(mine), other, on_chip(weight))


def near_places(table, slot, refs):
    x, c = (table[72], table[73])
    region = region_of(slot, x, c)
    places = []
    for side, ref in refs:
        for step in range(3):
            near = jnp.clip(region + step - 1, 0, 7)
            flag = table[region * 9 + step * 3 + side]
            places.append((ref, slot_of(near, x, c), jnp.where(flag > 0, 0.0, 1e30).astype(F32)))
    return places


def run_units(table, query_ref, refs, score_ref, weight_ref, known_top, finish):
    lanes = lax.broadcasted_iota(jnp.int32, (256, 128), 1)
    units = []
    for place in range(4):
        places = near_places(table, pl.program_id(0) * 4 + place, refs)
        for head in range(2):
            inside = (lanes >= head * 64) & (lanes < head * 64 + 64)
            query = jnp.where(inside, query_ref[place], jnp.zeros((), BF16))
            units.append((place, head, places, query))
    count = len(units[0][2])
    ones = jnp.ones((16, count * 256), BF16)
    tops = []
    for turn in range(9):
        column_tops = []
        for entry in range(count):
            rows = slice(entry * 256, entry * 256 + 256)
            if turn < 8:
                _, _, places, query = units[turn]
                ref, slot, penalty = places[entry]
                scores = lax.dot_general(
                    ref[slot, 0:256, :], query, (((1,), (1,)), ((), ())),
                    preferred_element_type=F32,
                )
                score_ref[turn % 2, rows] = scores
                column_tops.append(jnp.max(scores, axis=0, keepdims=True) - penalty)
            if turn > 0:
                penalty = units[turn - 1][2][entry][2]
                weight_ref[(turn - 1) % 2, rows] = jnp.exp2(
                    score_ref[(turn - 1) % 2, rows] - (tops[-1] + penalty)
                ).astype(BF16)
        if turn > 0:
            place, head, places, _ = units[turn - 1]
            halves = []
            for ref, slot, _ in places:
                halves.append(ref[slot, 256 + head * 64 : 320 + head * 64, :])
                halves.append(ref[slot, 384 + head * 64 : 448 + head * 64, :])
            values = jnp.concatenate([jnp.concatenate(halves, axis=1), ones], axis=0)
            total = jnp.dot(values, weight_ref[(turn - 1) % 2], preferred_element_type=F32)
            finish(place, head, tops[-1], total)
        if turn < 8:
            top = functools.reduce(jnp.maximum, column_tops)
            if known_top is not None:
                top = jnp.maximum(top, known_top(*units[turn][:2]))
            tops.append(top)


def attend_own_kernel(
    table, query_ref, own_ref, total_ref, top_ref, score_ref, weight_ref
):
    def finish(place, head, top, total):
        total_ref[place, head] = total
        top_ref[place, head] = jnp.broadcast_to(top, (8, 256))

    run_units(table, query_ref, [(1, own_ref)], score_ref, weight_ref, None, finish)


def attend_own(table, queries, own):
    return pl.pallas_call(
        attend_own_kernel,
        grid_spec=pltpu.PrefetchScalarGridSpec(
            num_scalar_prefetch=1,
            grid=(2,),
            in_specs=[pl.BlockSpec((4, 256, 128), lambda s, t: (s, 0, 0)), WHOLE],
            out_specs=[
                pl.BlockSpec((4, 2, 80, 256), lambda s, t: (s, 0, 0, 0)),
                pl.BlockSpec((4, 2, 8, 256), lambda s, t: (s, 0, 0, 0)),
            ],
            scratch_shapes=[pltpu.VMEM((2, 768, 256), F32), pltpu.VMEM((2, 768, 256), BF16)],
        ),
        out_shape=[
            jax.ShapeDtypeStruct((8, 2, 80, 256), F32),
            jax.ShapeDtypeStruct((8, 2, 8, 256), F32),
        ],
        name="attend_own",
    )(table, queries, own)


def attend_kernel(
    table, query_ref, low_ref, high_ref, own_total_ref, own_top_ref, out_ref, score_ref, weight_ref
):
    def known_top(place, head):
        return own_top_ref[place, head, 0:1]

    def finish(place, head, top, total):
        total += own_total_ref[place, head] * jnp.exp2(known_top(place, head) - top)
        region = region_of(pl.program_id(0) * 4 + place, table[72], table[73])
        out_ref[region, head * 64 : head * 64 + 64, :] = (total[:64] / total[64:65]).astype(BF16)

    run_units(table, query_ref, [(0, low_ref), (2, high_ref)], score_ref, weight_ref, known_top, finish)


def attend(table, queries, low, high, own_total, own_top):
    return pl.pallas_call(
        attend_kernel,
        grid_spec=pltpu.PrefetchScalarGridSpec(
            num_scalar_prefetch=1,
            grid=(2,),
            in_specs=[
                pl.BlockSpec((4, 256, 128), lambda s, t: (s, 0, 0)),
                WHOLE,
                WHOLE,
                pl.BlockSpec((4, 2, 80, 256), lambda s, t: (s, 0, 0, 0)),
                pl.BlockSpec((4, 2, 8, 256), lambda s, t: (s, 0, 0, 0)),
            ],
            out_specs=pl.BlockSpec((8, 128, 256), lambda s, t: (0, 0, 0)),
            scratch_shapes=[pltpu.VMEM((2, 1536, 256), F32), pltpu.VMEM((2, 1536, 256), BF16)],
        ),
        out_shape=jax.ShapeDtypeStruct((8, 128, 256), BF16),
        name="attend",
    )(table, queries, on_chip(low), on_chip(high), own_total, own_top)


def output_kernel(table, mixed_ref, mine_ref, other_ref, voxels_ref, out_ref):
    rows = [r * 128 + y * 16 for y in range(8) for r in range(8)]
    mixed = jnp.concatenate([mixed_ref[row : row + 16, :] for row in rows], axis=0).T
    c = table[73]
    for chip in range(4):
        weight = jnp.concatenate([mine_ref[chip], other_ref[chip]], axis=1)
        projected = jnp.dot(mixed, weight, preferred_element_type=F32)
        for place, parity in enumerate((c, 1 - c)):
            cols = pl.ds(pl.multiple_of(chip * 256 + parity * 128, 128), 128)
            part = projected[:, place * 128 : place * 128 + 128]
            out_ref[:, cols] = (voxels_ref[:, cols].astype(F32) + part).astype(BF16)


def project_out(table, mixed, mine, other, voxels):
    return pl.pallas_call(
        output_kernel,
        grid_spec=pltpu.PrefetchScalarGridSpec(
            num_scalar_prefetch=1,
            grid=(1,),
            in_specs=[
                pl.BlockSpec(memory_space=pltpu.VMEM),
                pl.BlockSpec((4, 1024, 128), lambda n, t: (0, 0, 0)),
                pl.BlockSpec(memory_space=pltpu.VMEM),
                pl.BlockSpec((256, 1024), lambda n, t: (0, 0)),
            ],
            out_specs=pl.BlockSpec((256, 1024), lambda n, t: (0, 0)),
        ),
        out_shape=jax.ShapeDtypeStruct((256, 1024), BF16),
        name="project_out",
    )(table, on_chip(mixed), mine, on_chip(other), voxels)


def gathered_line(value):
    pieces = [value]
    for step in (1, -1, 2):
        pieces.append(shift(value, "x", step))
    mine = jnp.concatenate(pieces, axis=0)
    return (mine, shift(mine, "c", 1))


def layer(voxels, norm_gain, qkv_weight, out_weight, neighbours):
    x, c, z = (lax.axis_index(a) for a in ("x", "c", "z"))
    tokens = voxels.reshape(256, 1024)
    normed, parts = prepare(
        neighbours.reshape(1, 8), tokens, norm_gain.reshape(1, 1024), qkv_weight, out_weight
    )
    mine, other = gathered_line(normed)

    swapped = lax.all_to_all(parts, ("x", "c", "z"), 0, 0, tiled=True)
    masks = lax.dynamic_index_in_dim(swapped.reshape(8, 8, 2, 640), z, 1, keepdims=False)
    table = jnp.concatenate([
        masks[:, 0, 512:521].astype(jnp.int32).reshape(72),
        jnp.stack([x, c]).astype(jnp.int32),
    ])
    swapped = swapped.reshape(128, 640)

    weight = from_everyone(swapped[:, :384], "y")
    own, queries = project_qkv(mine, other, weight)
    line = [(i, i + 1) for i in range(63)]
    low = lax.ppermute(own, PLANE, line)
    high = lax.ppermute(own, PLANE, [(j, i) for i, j in line])

    out_part, _ = lax.optimization_barrier((swapped[:, 384:512], queries))
    out_part = from_everyone(out_part, "y").reshape(1024, 128)
    own_total, own_top = attend_own(table, queries, own)
    out_mine = from_everyone(out_part, "x")
    out_other = shift(out_mine, "c", 1)
    mixed = attend(table, queries, low, high, own_total, own_top)
    mixed = lax.all_to_all(mixed, LINE, 0, 0, tiled=True).reshape(1024, 256)
    result = project_out(table, mixed, out_mine, out_other, tokens)
    return result.reshape(voxels.shape)


def solution(mesh):
    fine = Mesh(mesh.devices.reshape(4, 2, 8, 8), ("x", "c", "y", "z"))
    return jax.shard_map(
        layer,
        mesh=fine,
        in_specs=(
            P(LINE, PLANE, None, None, None),
            P(),
            P((*LINE, *PLANE), None),
            P((*LINE, *PLANE), None),
            P(LINE, PLANE, None, None),
        ),
        out_specs=P(LINE, PLANE, None, None, None),
        check_vma=False,
    )
```

```python
import functools

import jax
import jax.numpy as jnp
from jax import lax
from jax.experimental import pallas as pl
from jax.experimental.pallas import tpu as pltpu
from jax.sharding import Mesh, PartitionSpec as P


HEAD_DIM = 64
FACTOR = HEAD_DIM ** (-0.5) * 1.4426950408889634
LINE = ("x", "c")
PLANE = ("y", "z")
BF16 = jnp.bfloat16
F32 = jnp.float32


def norm(tokens_ref, gain_ref, out_ref):
    widened = tokens_ref[...].astype(F32)
    average = jnp.mean(widened, axis=-1, keepdims=True)
    centred = widened - average
    spread = jnp.mean(centred * centred, axis=-1, keepdims=True)
    out_ref[...] = (centred * lax.rsqrt(spread + 1e-06) * gain_ref[...]).astype(BF16)


def prepare_kernel(
    lists_ref, tokens_ref, gain_ref, weight_ref, out_weight_ref, normed_ref, messages_ref
):
    norm(tokens_ref, gain_ref, normed_ref)

    @pl.when(pl.program_id(0) == 0)
    def _():
        write_messages(lists_ref, weight_ref, out_weight_ref, messages_ref)


def write_messages(lists_ref, weight_ref, out_weight_ref, out_ref):
    region = 2 * lax.axis_index("x") + lax.axis_index("c")
    owner = 8 * lax.axis_index("y") + lax.axis_index("z")
    lanes = lax.broadcasted_iota(jnp.int32, (2, 128), 1)
    flags = jnp.where(lanes == 4, 1.0, 0.0)
    for entry in (0, 1, 2, 3, 5, 6, 7, 8):
        near_region = region + entry // 3 - 1
        near_owner = owner + entry % 3 - 1
        inside = (
            (near_region >= 0) & (near_region < 8) & (near_owner >= 0) & (near_owner < 64)
        )
        number = jnp.where(inside, near_region * 64 + near_owner, -2)
        listed = functools.reduce(jnp.logical_or, [lists_ref[0, i] == number for i in range(8)])
        flags = jnp.where((lanes == entry) & listed, 1.0, flags)
    flags = flags.astype(BF16)
    for head_pair in range(8):
        start = head_pair * 128
        parts = [weight_ref[:, base + start : base + start + 128] for base in (1024, 2048, 0)]
        parts += [out_weight_ref[:, start : start + 128], flags]
        message = jnp.concatenate(parts, axis=1)
        for z in range(8):
            out_ref[head_pair * 8 + z] = message


def prepare(lists, tokens, gain, weight, out_weight):
    return pl.pallas_call(
        prepare_kernel,
        grid=(2,),
        in_specs=[
            pl.BlockSpec(memory_space=pltpu.SMEM),
            pl.BlockSpec((128, 1024), lambda i: (i, 0)),
            pl.BlockSpec((1, 1024), lambda i: (0, 0)),
            pl.BlockSpec((2, 3072), lambda i: (0, 0)),
            pl.BlockSpec((2, 1024), lambda i: (0, 0)),
        ],
        out_specs=[
            pl.BlockSpec((128, 1024), lambda i: (i, 0)),
            pl.BlockSpec((64, 2, 640), lambda i: (0, 0, 0)),
        ],
        out_shape=[
            jax.ShapeDtypeStruct((256, 1024), BF16),
            jax.ShapeDtypeStruct((64, 2, 640), BF16),
        ],
        name="prepare",
    )(lists, tokens, gain, weight, out_weight)


def shift(value, axis, step):
    n = lax.axis_size(axis)
    return lax.ppermute(value, axis, [(i, (i + step) % n) for i in range(n)])


def from_everyone(value, axes):
    n = lax.axis_size(axes)
    return lax.all_to_all(jnp.broadcast_to(value[None], (n, *value.shape)), axes, 0, 0, tiled=True)


def region_of(slot, x, c):
    parity, place = (slot // 4, slot % 4)
    step = jnp.where(place == 0, 0, jnp.where(place == 1, 3, place - 1))
    return 2 * ((x + step) % 4) + (c + parity) % 2


def slot_of(region, x, c):
    step = (region // 2 - x + 4) % 4
    place = jnp.where(step == 0, 0, jnp.where(step == 3, 1, step + 1))
    return 4 * ((region % 2 + c) % 2) + place


WHOLE = pl.BlockSpec(memory_space=pltpu.VMEM)


def on_chip(value):
    return pltpu.with_memory_space_constraint(value, pltpu.VMEM)


def qkv_kernel(mine_ref, other_ref, gathered_ref, kv_ref, query_ref, weight_ref):
    @pl.when(pl.program_id(0) == 0)
    def _():
        for region in range(8):
            for y in range(8):
                row = region * 128 + y * 16
                weight_ref[row : row + 16] = gathered_ref[y, region * 16 : region * 16 + 16]

    def project(tokens):
        projected = jnp.dot(tokens, weight_ref[...], preferred_element_type=F32)
        for block in range(2):
            rows = slice(block * 256, block * 256 + 256)
            kv_ref[block, 0:256, :] = projected[rows, :128].astype(BF16)
            values = projected[rows, 128:256].astype(BF16).T
            kv_ref[block, 256:384, :] = values[:, :128]
            kv_ref[block, 384:512, :] = values[:, 128:]
            query_ref[block] = (projected[rows, 256:] * FACTOR).astype(BF16)

    @pl.when(pl.program_id(0) < 2)
    def _():
        project(mine_ref[pl.ds(pl.multiple_of(pl.program_id(0) * 512, 512), 512), :])

    @pl.when(pl.program_id(0) >= 2)
    def _():
        project(other_ref[...])


def project_qkv(mine, other, weight):
    return pl.pallas_call(
        qkv_kernel,
        grid=(4,),
        in_specs=[
            pl.BlockSpec(memory_space=pltpu.VMEM),
            pl.BlockSpec((512, 1024), lambda s: (jnp.maximum(s - 2, 0), 0)),
            pl.BlockSpec(memory_space=pltpu.VMEM),
        ],
        out_specs=[
            pl.BlockSpec((2, 512, 128), lambda s: (s, 0, 0)),
            pl.BlockSpec((2, 256, 128), lambda s: (s, 0, 0)),
        ],
        out_shape=[
            jax.ShapeDtypeStruct((8, 512, 128), BF16),
            jax.ShapeDtypeStruct((8, 256, 128), BF16),
        ],
        scratch_shapes=[pltpu.VMEM((1024, 384), BF16)],
        name="project_qkv",
    )(on_chip(mine), other, on_chip(weight))


def near_places(table, slot, refs):
    x, c = (table[72], table[73])
    region = region_of(slot, x, c)
    places = []
    for side, ref in refs:
        for step in range(3):
            near = jnp.clip(region + step - 1, 0, 7)
            flag = table[region * 9 + step * 3 + side]
            places.append((ref, slot_of(near, x, c), jnp.where(flag > 0, 0.0, 1e30).astype(F32)))
    return places


def run_units(table, query_ref, refs, score_ref, weight_ref, known_top, finish):
    lanes = lax.broadcasted_iota(jnp.int32, (256, 128), 1)
    units = []
    for place in range(4):
        places = near_places(table, pl.program_id(0) * 4 + place, refs)
        for head in range(2):
            inside = (lanes >= head * 64) & (lanes < head * 64 + 64)
            query = jnp.where(inside, query_ref[place], jnp.zeros((), BF16))
            units.append((place, head, places, query))
    count = len(units[0][2])
    ones = jnp.ones((16, count * 256), BF16)
    tops = []
    for turn in range(9):
        column_tops = []
        for entry in range(count):
            rows = slice(entry * 256, entry * 256 + 256)
            if turn < 8:
                _, _, places, query = units[turn]
                ref, slot, penalty = places[entry]
                scores = lax.dot_general(
                    ref[slot, 0:256, :], query, (((1,), (1,)), ((), ())),
                    preferred_element_type=F32,
                )
                score_ref[turn % 2, rows] = scores
                column_tops.append(jnp.max(scores, axis=0, keepdims=True) - penalty)
            if turn > 0:
                penalty = units[turn - 1][2][entry][2]
                weight_ref[(turn - 1) % 2, rows] = jnp.exp2(
                    score_ref[(turn - 1) % 2, rows] - (tops[-1] + penalty)
                ).astype(BF16)
        if turn > 0:
            place, head, places, _ = units[turn - 1]
            halves = []
            for ref, slot, _ in places:
                halves.append(ref[slot, 256 + head * 64 : 320 + head * 64, :])
                halves.append(ref[slot, 384 + head * 64 : 448 + head * 64, :])
            values = jnp.concatenate([jnp.concatenate(halves, axis=1), ones], axis=0)
            total = jnp.dot(values, weight_ref[(turn - 1) % 2], preferred_element_type=F32)
            finish(place, head, tops[-1], total)
        if turn < 8:
            top = functools.reduce(jnp.maximum, column_tops)
            if known_top is not None:
                top = jnp.maximum(top, known_top(*units[turn][:2]))
            tops.append(top)


def attend_own_kernel(
    table, query_ref, own_ref, total_ref, top_ref, score_ref, weight_ref
):
    def finish(place, head, top, total):
        total_ref[place, head] = total
        top_ref[place, head] = jnp.broadcast_to(top, (8, 256))

    run_units(table, query_ref, [(1, own_ref)], score_ref, weight_ref, None, finish)


def attend_own(table, queries, own):
    return pl.pallas_call(
        attend_own_kernel,
        grid_spec=pltpu.PrefetchScalarGridSpec(
            num_scalar_prefetch=1,
            grid=(2,),
            in_specs=[pl.BlockSpec((4, 256, 128), lambda s, t: (s, 0, 0)), WHOLE],
            out_specs=[
                pl.BlockSpec((4, 2, 80, 256), lambda s, t: (s, 0, 0, 0)),
                pl.BlockSpec((4, 2, 8, 256), lambda s, t: (s, 0, 0, 0)),
            ],
            scratch_shapes=[pltpu.VMEM((2, 768, 256), F32), pltpu.VMEM((2, 768, 256), BF16)],
        ),
        out_shape=[
            jax.ShapeDtypeStruct((8, 2, 80, 256), F32),
            jax.ShapeDtypeStruct((8, 2, 8, 256), F32),
        ],
        name="attend_own",
    )(table, queries, own)


def attend_kernel(
    table, query_ref, low_ref, high_ref, own_total_ref, own_top_ref, out_ref, score_ref, weight_ref
):
    def known_top(place, head):
        return own_top_ref[place, head, 0:1]

    def finish(place, head, top, total):
        total += own_total_ref[place, head] * jnp.exp2(known_top(place, head) - top)
        region = region_of(pl.program_id(0) * 4 + place, table[72], table[73])
        out_ref[region, head * 64 : head * 64 + 64, :] = (total[:64] / total[64:65]).astype(BF16)

    run_units(table, query_ref, [(0, low_ref), (2, high_ref)], score_ref, weight_ref, known_top, finish)


def attend(table, queries, low, high, own_total, own_top):
    return pl.pallas_call(
        attend_kernel,
        grid_spec=pltpu.PrefetchScalarGridSpec(
            num_scalar_prefetch=1,
            grid=(2,),
            in_specs=[
                pl.BlockSpec((4, 256, 128), lambda s, t: (s, 0, 0)),
                WHOLE,
                WHOLE,
                pl.BlockSpec((4, 2, 80, 256), lambda s, t: (s, 0, 0, 0)),
                pl.BlockSpec((4, 2, 8, 256), lambda s, t: (s, 0, 0, 0)),
            ],
            out_specs=pl.BlockSpec((8, 128, 256), lambda s, t: (0, 0, 0)),
            scratch_shapes=[pltpu.VMEM((2, 1536, 256), F32), pltpu.VMEM((2, 1536, 256), BF16)],
        ),
        out_shape=jax.ShapeDtypeStruct((8, 128, 256), BF16),
        name="attend",
    )(table, queries, on_chip(low), on_chip(high), own_total, own_top)


def output_kernel(table, mixed_ref, mine_ref, other_ref, voxels_ref, out_ref):
    rows = [r * 128 + y * 16 for y in range(8) for r in range(8)]
    mixed = jnp.concatenate([mixed_ref[row : row + 16, :] for row in rows], axis=0).T
    c = table[73]
    for chip in range(4):
        weight = jnp.concatenate([mine_ref[chip], other_ref[chip]], axis=1)
        projected = jnp.dot(mixed, weight, preferred_element_type=F32)
        for place, parity in enumerate((c, 1 - c)):
            cols = pl.ds(pl.multiple_of(chip * 256 + parity * 128, 128), 128)
            part = projected[:, place * 128 : place * 128 + 128]
            out_ref[:, cols] = (voxels_ref[:, cols].astype(F32) + part).astype(BF16)


def project_out(table, mixed, mine, other, voxels):
    return pl.pallas_call(
        output_kernel,
        grid_spec=pltpu.PrefetchScalarGridSpec(
            num_scalar_prefetch=1,
            grid=(1,),
            in_specs=[
                pl.BlockSpec(memory_space=pltpu.VMEM),
                pl.BlockSpec((4, 1024, 128), lambda n, t: (0, 0, 0)),
                pl.BlockSpec(memory_space=pltpu.VMEM),
                pl.BlockSpec((256, 1024), lambda n, t: (0, 0)),
            ],
            out_specs=pl.BlockSpec((256, 1024), lambda n, t: (0, 0)),
        ),
        out_shape=jax.ShapeDtypeStruct((256, 1024), BF16),
        name="project_out",
    )(table, on_chip(mixed), mine, on_chip(other), voxels)


def gathered_line(value, after):
    own, _ = lax.optimization_barrier((value, after))
    pieces = [own]
    for step in (1, -1, 2):
        pieces.append(shift(value, "x", step))
    mine = jnp.concatenate(pieces, axis=0)
    return (mine, shift(mine, "c", 1))


def layer(voxels, norm_gain, qkv_weight, out_weight, neighbours):
    x, c, z = (lax.axis_index(a) for a in ("x", "c", "z"))
    tokens = voxels.reshape(256, 1024)
    normed, parts = prepare(
        neighbours.reshape(1, 8), tokens, norm_gain.reshape(1, 1024), qkv_weight, out_weight
    )

    swapped = lax.all_to_all(parts, ("x", "c", "z"), 0, 0, tiled=True)
    masks = lax.dynamic_index_in_dim(swapped.reshape(8, 8, 2, 640), z, 1, keepdims=False)
    table = jnp.concatenate([
        masks[:, 0, 512:521].astype(jnp.int32).reshape(72),
        jnp.stack([x, c]).astype(jnp.int32),
    ])
    swapped = swapped.reshape(128, 640)

    weight = from_everyone(swapped[:, :384], "y")
    mine, other = gathered_line(normed, swapped)
    own, queries = project_qkv(mine, other, weight)
    line = [(i, i + 1) for i in range(63)]
    low = lax.ppermute(own, PLANE, line)
    high = lax.ppermute(own, PLANE, [(j, i) for i, j in line])

    out_part, _ = lax.optimization_barrier((swapped[:, 384:512], queries))
    out_part = from_everyone(out_part, "y").reshape(1024, 128)
    own_total, own_top = attend_own(table, queries, own)
    out_mine = from_everyone(out_part, "x")
    out_other = shift(out_mine, "c", 1)
    mixed = attend(table, queries, low, high, own_total, own_top)
    mixed = lax.all_to_all(mixed, LINE, 0, 0, tiled=True).reshape(1024, 256)
    result = project_out(table, mixed, out_mine, out_other, tokens)
    return result.reshape(voxels.shape)


def solution(mesh):
    fine = Mesh(mesh.devices.reshape(4, 2, 8, 8), ("x", "c", "y", "z"))
    return jax.shard_map(
        layer,
        mesh=fine,
        in_specs=(
            P(LINE, PLANE, None, None, None),
            P(),
            P((*LINE, *PLANE), None),
            P((*LINE, *PLANE), None),
            P(LINE, PLANE, None, None),
        ),
        out_specs=P(LINE, PLANE, None, None, None),
        check_vma=False,
    )
```
